512 devices in a mesh: row: 16 (over z_lo, x), col: 32 (over y, z_hi, core).
Axes of the slice: x: 4, y: 4, z: 16 (z_hi: 4, z_lo: 4; z = z_hi * 4 + z_lo), core: 2. Of those that a mesh axis runs over, the one named last changes fastest.
Arguments:
- alignment: int32 [512, 480], P(None, 'row'), may hold values from 0 to 20
- seq_weight: float32 [512], replicated, may hold values from 0.1 to 1
- couplings: float32 [10080, 10080], P('row', 'col'), may hold values from -0.15 to 0.15, as said below
- pair_mean: float32 [10080, 10080], P('row', 'col'), may hold values from -4 to 4, as said below
- pair_square: float32 [10080, 10080], P('row', 'col'), may hold values from 1 to 100, as said below
- fields: float32 [10080], P('row'), may hold values from -2 to 2
- field_mean: float32 [10080], P('row'), may hold values from -4 to 4
- field_square: float32 [10080], P('row'), may hold values from 1 to 100
Outputs:
- updated_pairs: float32 [10080, 10080], P('row', 'col')
- updated_pair_mean: float32 [10080, 10080], P('row', 'col')
- updated_pair_square: float32 [10080, 10080], P('row', 'col')
- updated_fields: float32 [10080], P('row')
- updated_field_mean: float32 [10080], P('row')
- updated_field_square: float32 [10080], P('row')
The draws below stay inside these ranges and needn't reach their ends.
Inputs may be any that keep to these rules, and one draw needn't show every extreme that they name: alignment holds whole numbers below 21; a program may send them packed, several to one 32-bit word. couplings is symmetric (entry (k, m) equals entry (m, k)); entries whose row and column belong to the same residue (k // 21 == m // 21) are zero. pair_mean is symmetric; entries whose row and column belong to the same residue are zero. pair_square is symmetric.
All inputs are finite; a program needn't handle non-finite values.
Results may differ from the reference program's by a relative error of at most 0.00005.
Values sent between devices are 32-bit elements; how exact they have to be, the bound alone decides.
A program may use at most 64 MiB of HBM per device.

```python
import math
import jax
import jax.numpy as jnp
from jax import lax

L = 480
Q = 21
SEQS = 512


def mirror_mean(values):
    return 0.5 * (values + values.T)


def residue_mask():
    residue = jnp.arange(L * Q, dtype=jnp.int32) // Q
    return residue[:, None] != residue[None, :]


def draw_couplings(key, part):
    key = jax.random.fold_in(key, 11)
    raw_values = jnp.clip(0.05 * jax.random.normal(key, (L * Q, L * Q), jnp.float32), -0.15, 0.15)
    mixed = mirror_mean(raw_values)
    return jnp.where(residue_mask(), mixed, 0.0).astype(jnp.float32)


def draw_pair_mean(key, part):
    key = jax.random.fold_in(key, 23)
    raw_values = jnp.clip(jax.random.normal(key, (L * Q, L * Q), jnp.float32), -4.0, 4.0)
    return jnp.where(residue_mask(), mirror_mean(raw_values), 0.0).astype(jnp.float32)


def draw_pair_square(key, part):
    key = jax.random.fold_in(key, 37)
    logs = jax.random.uniform(key, (L * Q, L * Q), jnp.float32, 0.0, 4.6051702)
    return jnp.clip(jnp.exp(mirror_mean(logs)), 1.0, 100.0).astype(jnp.float32)


def plant(values, stream_key, low, top_value):
    index_at = [jax.random.randint(jax.random.fold_in(stream_key, axis), (), 0, length) for axis, length in enumerate(values.shape)]
    main_axis = values.shape.index(max(values.shape))
    next_to = index_at[:main_axis] + [(index_at[main_axis] + 1) % values.shape[main_axis]] + index_at[main_axis + 1:]
    return values.at[tuple(index_at)].set(low).at[tuple(next_to)].set(top_value)


def block_levels(rng, dims, shards, low, high):
    loudness, own = 1.0, jax.random.fold_in(rng, 6)
    for axis_at, blocks in shards:
        heights = jnp.exp(jax.random.uniform(jax.random.fold_in(own, axis_at), (blocks,), jnp.float32, low / len(shards), high / len(shards)))
        loudness = loudness * jnp.repeat(heights, dims[axis_at] // blocks).reshape([-1 if axis == axis_at else 1 for axis in range(len(dims))])
    return loudness


def scatter_about(key, dims, spread, bound, split=(), held_as=jnp.bfloat16):
    level = block_levels(key, dims, split, -0.22, 0.18) if split else 1.0
    entries = jax.random.normal(key, dims, jnp.float32) * spread * level
    return jnp.minimum(jnp.maximum(entries, -bound), bound).astype(held_as)


def setup_inputs(seed: int = 0) -> dict:
    keys = jax.random.split(jax.random.key(seed), 9)
    return {
        "alignment": plant(jax.random.randint(keys[0], (SEQS, L), 0, Q), jax.random.fold_in(keys[0], 1), 0, Q - 1).astype(jnp.int32),
        "seq_weight": jnp.clip(jnp.exp(jax.random.uniform(keys[1], (SEQS,), jnp.float32, math.log(0.1), math.log(1.0))), 0.1, 1.0),
        "couplings": draw_couplings(jax.random.fold_in(keys[8], 71), 0),
        "pair_mean": draw_pair_mean(jax.random.fold_in(keys[8], 71), 0),
        "pair_square": draw_pair_square(jax.random.fold_in(keys[8], 71), 0),
        "fields": jnp.clip(jax.random.uniform(keys[5], (L * Q,), jnp.float32, -2.0, 2.0) * block_levels(keys[5], (L * Q,), ((0, 16),), -0.4, 0.0), -2.0, 2.0),
        "field_mean": scatter_about(keys[6], (L * Q,), 1.0, 4.0, ((0, 16),), jnp.float32),
        "field_square": jnp.clip(jnp.exp(math.log(100.0) - 4.6051702 * jax.random.uniform(keys[7], (L * Q,), jnp.float32) ** block_levels(keys[7], (L * Q,), ((0, 16),), -0.2, 0.2)), 1.0, 100.0),
    }


def encode_states(states):
    levels = jnp.arange(Q, dtype=jnp.int32)
    encoded = (states[:, :, None] == levels[None, None, :]).astype(jnp.float32)
    return encoded.reshape(states.shape[0], states.shape[1] * Q)

def adam_update(values, first_moment, second_moment, gradient):
    first_new = 0.9 * first_moment + 0.1 * gradient
    second_new = 0.999 * second_moment + 0.001 * gradient * gradient
    change = 0.05 * (first_new / (1.0 - 0.9 ** 10)) / (jnp.sqrt(second_new / (1.0 - 0.999 ** 10)) + 1e-08)
    return (values - change, first_new, second_new)

def reference(alignment, seq_weight, couplings, pair_mean, pair_square, fields, field_mean, field_square):
    onehot = encode_states(alignment)
    energy = jnp.dot(onehot, couplings.T, precision=lax.Precision.HIGHEST, preferred_element_type=jnp.float32) + fields[None, :]
    powers = jnp.exp(energy).reshape(SEQS, L, Q)
    prob = (powers / lax.optimization_barrier(jnp.sum(powers, axis=2, keepdims=True))).reshape(SEQS, L * Q)
    weighted = seq_weight[:, None] * (prob - onehot)
    half = jnp.dot(weighted.T, onehot, precision=lax.Precision.HIGHEST, preferred_element_type=jnp.float32)
    residue = jnp.arange(L * Q, dtype=jnp.int32) // Q
    off_diagonal = residue[:, None] != residue[None, :]
    pair_grad = jnp.where(off_diagonal, half + half.T, 0.0) + 0.2 * (L - 1) * couplings
    field_grad = lax.optimization_barrier(jnp.sum(weighted, axis=0))
    new_pairs, new_pair_mean, new_pair_square = adam_update(couplings, pair_mean, pair_square, pair_grad)
    new_fields, new_field_mean, new_field_square = adam_update(fields, field_mean, field_square, field_grad)
    return (new_pairs, new_pair_mean, new_pair_square, new_fields, new_field_mean, new_field_square)
```

```python
import jax
import jax.numpy as jnp
from jax import lax
from jax.experimental import pallas as pl
from jax.experimental.pallas import tpu as pltpu
from jax.sharding import PartitionSpec as P

L = 480
Q = 21
MESH = pl.DeviceIdType.MESH
F32 = jnp.float32
BF16 = jnp.bfloat16


def two_parts(x):
    high = x.astype(BF16)
    return high, (x - high.astype(F32)).astype(BF16)


def three_parts(x):
    high = x.astype(BF16)
    rest = x - high.astype(F32)
    mid = rest.astype(BF16)
    return high, mid, (rest - mid.astype(F32)).astype(BF16)


def dot(a, b, dims=((1,), (0,))):
    return lax.dot_general(a, b, (dims, ((), ())), preferred_element_type=F32)


def residue_of(lane):
    return ((lane.astype(F32) + 0.5) * (1.0 / Q)).astype(jnp.int32)


def flip(i):
    return i + 1 - 2 * (i % 2)


def mirror(i):
    return 3 - i


def packed_column(lane):
    main = jnp.where(lane < 256, lane, lane - 256)
    tail = jnp.where(lane < 576, lane - 512, lane - 576)
    column = jnp.where(lane < 512, main, tail + 256)
    second = ((lane >= 256) & (lane < 512)) | (lane >= 576)
    return column, second, (lane < 512) | (tail < 59)


def kernel(
    al_ref, w_ref, j_ref, f_ref, g_ref, fg_ref,
    states, oc32, or32, j_high, j_low, part, got, xr, xc,
    r_in1, r_in2, r_in3, r_in4, c_in1, c_in2, c_in3, c_in4, wr, wc, acc,
    fpad, state_send, send, recv,
):
    row, col = lax.axis_index("row"), lax.axis_index("col")
    z_lo, x = row // 4, row % 4
    y, z_hi, core = col // 8, (col // 2) % 4, col % 2
    owner = col // 2

    def at_row(a, b):
        return (row, a * 8 + b * 2 + core)

    def at_col(a, b):
        return (b * 4 + a, col)

    partner = (row, y * 8 + z_hi * 2 + 1 - core)

    barrier = pltpu.get_barrier_semaphore()
    greeted = [at_row(flip(y), z_hi), at_row(mirror(y), z_hi), at_row(y, flip(z_hi))]
    greeted += [at_row(y, mirror(z_hi)), partner]
    greeted += [((row + d) % 16, col) for d in range(1, 16)]
    for device in greeted:
        pl.semaphore_signal(barrier, inc=1, device_id=device, device_id_type=MESH)

    fpad[...] = jnp.zeros_like(fpad)
    fpad[0:1, 0:630] = f_ref[...]
    alignment = al_ref[...].astype(F32).astype(BF16)
    pick_row = lax.broadcasted_iota(jnp.int32, (16, 30), 0)
    pick_col = lax.broadcasted_iota(jnp.int32, (16, 30), 1)
    pick = (pick_col == pick_row + 15 * core) & (pick_row < 15)
    own_states = dot(pick.astype(F32).astype(BF16), alignment, ((1,), (1,)))

    pl.semaphore_wait(barrier, len(greeted))

    state_copies = [
        pltpu.make_async_remote_copy(
            states, states, state_send.at[d], recv.at[0],
            device_id=((row + d) % 16, col), device_id_type=MESH,
        )
        for d in range(1, 16)
    ]

    @pl.when(row == owner)
    def _():
        states[...] = own_states
        fields = fpad[...]
        moved = jnp.where(core == 0, fields, pltpu.roll(fields, 325, 1))
        field_lane = lax.broadcasted_iota(jnp.int32, (1, 512), 1)
        states[15:16, :] = jnp.where(field_lane < 315, moved[0:1, 0:512], 0.0)
        for copy in state_copies:
            copy.start()

    copies = []

    def exchange(src, dst, device):
        at = len(copies) + 1
        copy = pltpu.make_async_remote_copy(
            src, dst, send.at[at], recv.at[at], device_id=device, device_id_type=MESH
        )
        copy.start()
        copies.append(copy)
        return copy

    j_high[...] = jnp.zeros_like(j_high)
    j_low[...] = jnp.zeros_like(j_low)
    high, low = two_parts(j_ref[...])
    j_high[0:630, 0:315] = high
    j_low[0:630, 0:315] = low

    lane_r = lax.broadcasted_iota(jnp.int32, (1, 640), 1)
    res_r = residue_of(lane_r)
    spread_r = lax.broadcasted_iota(jnp.int32, (30, 640), 0) == residue_of(
        lax.broadcasted_iota(jnp.int32, (30, 640), 1)
    )
    value_r = dot(alignment, spread_r.astype(F32).astype(BF16))
    hot_r = (value_r == (lane_r - res_r * Q).astype(F32)) & (lane_r < 630)
    hot_r = hot_r.astype(F32)
    or32[...] = hot_r.reshape(64, 8, 640)
    hot_r = hot_r.astype(BF16)

    top, bottom = hot_r[0:256], hot_r[256:512]
    tail_high, tail_low = j_high[:, 256:384], j_low[:, 256:384]
    tail_high2 = pltpu.roll(tail_high.astype(F32), 64, 1).astype(BF16)
    tail_low2 = pltpu.roll(tail_low.astype(F32), 64, 1).astype(BF16)
    main_high, main_low = j_high[:, 0:256], j_low[:, 0:256]
    xc[:, :, :, :, 0:256] = (dot(top, main_high) + dot(top, main_low)).reshape(4, 2, 4, 8, 256)
    xc[:, :, :, :, 256:512] = (dot(bottom, main_high) + dot(bottom, main_low)).reshape(4, 2, 4, 8, 256)
    xc[:, :, :, :, 512:640] = (
        dot(top, tail_high) + dot(top, tail_low) + dot(bottom, tail_high2) + dot(bottom, tail_low2)
    ).reshape(4, 2, 4, 8, 128)

    def order(i, half):
        first, second = flip(i), mirror(i)
        return (first, second) if half == 0 else (second, first)

    far = lambda i: (i + 2) % 4

    class Reduce:
        def __init__(self, a, b, at, total, in1, in2, in3, in4, full):
            self.a, self.b, self.at, self.total, self.full = a, b, at, total, full
            self.ins = (in1, in2, in3, in4)

        def step1(self):
            self.s1 = []
            for h in range(2):
                p, _ = order(self.a, h)
                to = self.at(p, self.b)
                self.s1.append([
                    exchange(self.total.at[p, h], self.ins[0].at[h, 0], to),
                    exchange(self.total.at[far(self.a), h], self.ins[0].at[h, 1], to),
                ])

        def step2(self):
            self.s2 = []
            for h in range(2):
                p, q = order(self.a, h)
                self.s1[h][1].wait_recv()
                self.total[q, h] += self.ins[0][h, 1]
                self.s2.append(exchange(self.total.at[q, h], self.ins[1].at[h], self.at(q, self.b)))
            for h in range(2):
                self.s1[h][0].wait_recv()
                self.total[self.a, h] += self.ins[0][h, 0]

        def step3(self):
            self.s3 = []
            for h in range(2):
                p, _ = order(self.b, h)
                self.s2[h].wait_recv()
                self.total[self.a, h] += self.ins[1][h]
                to = self.at(self.a, p)
                self.s3.append([
                    exchange(self.total.at[self.a, h, p], self.ins[2].at[h, 0], to),
                    exchange(self.total.at[self.a, h, far(self.b)], self.ins[2].at[h, 1], to),
                ])

        def step4(self):
            self.s4 = []
            for h in range(2):
                p, q = order(self.b, h)
                self.s3[h][1].wait_recv()
                self.total[self.a, h, q] += self.ins[2][h, 1]
                self.s4.append(
                    exchange(self.total.at[self.a, h, q], self.ins[3].at[h], self.at(self.a, q))
                )
            for h in range(2):
                self.s3[h][0].wait_recv()
                self.total[self.a, h, self.b] += self.ins[2][h, 0]

        def result(self):
            parts = []
            for h in range(2):
                self.s4[h].wait_recv()
                parts.append(self.total[self.a, h, self.b] + self.ins[3][h])
            return jnp.concatenate(parts, axis=0)

        def gather1(self, value):
            self.g1 = []
            for h in range(2):
                self.full[self.a, h, self.b] = value[8 * h : 8 * h + 8]
                _, q = order(self.b, h)
                own = self.full.at[self.a, h, self.b]
                self.g1.append(exchange(own, own, self.at(self.a, q)))

        def gather2(self):
            self.g2 = []
            for h in range(2):
                p, q = order(self.b, h)
                to = self.at(self.a, p)
                own, second = self.full.at[self.a, h, self.b], self.full.at[self.a, h, q]
                sent = [exchange(own, own, to)]
                self.g1[h].wait_recv()
                sent.append(exchange(second, second, to))
                self.g2.append(sent)

        def gather3(self):
            self.g3 = []
            for h in range(2):
                _, q = order(self.a, h)
                for copy in self.g2[h]:
                    copy.wait_recv()
                own = self.full.at[self.a, h]
                self.g3.append(exchange(own, own, self.at(q, self.b)))

        def gather4(self):
            self.g4 = []
            for h in range(2):
                p, q = order(self.a, h)
                to = self.at(p, self.b)
                own, second = self.full.at[self.a, h], self.full.at[q, h]
                sent = [exchange(own, own, to)]
                self.g3[h].wait_recv()
                sent.append(exchange(second, second, to))
                self.g4.append(sent)

        def gathered(self):
            for sent in self.g4:
                for copy in sent:
                    copy.wait_recv()

    cols = Reduce(x, z_lo, at_col, xc, c_in1, c_in2, c_in3, c_in4, wc)
    mine = wr.at[core]
    rows = Reduce(y, z_hi, at_row, xr, r_in1, r_in2, r_in3, r_in4, mine)
    cols.step1()

    @pl.when(row != owner)
    def _():
        state_copies[0].wait_recv()

    lane_c = lax.broadcasted_iota(jnp.int32, (1, 384), 1)
    spread_c = lax.broadcasted_iota(jnp.int32, (16, 384), 0) == residue_of(
        lax.broadcasted_iota(jnp.int32, (16, 384), 1)
    )
    state_rows = lax.broadcasted_iota(jnp.int32, (16, 512), 0)
    state_values = jnp.where(state_rows < 15, states[...], 0.0).astype(BF16)
    value_c = dot(state_values, spread_c.astype(F32).astype(BF16), ((0,), (0,)))
    hot_c = (value_c == (lane_c - residue_of(lane_c) * Q).astype(F32)) & (lane_c < 315)
    hot_c = hot_c.astype(F32)
    oc32[...] = hot_c.reshape(64, 8, 384)

    def row_part(which):
        lines = oc32[pl.ds(which * 32, 32)].reshape(256, 384).astype(BF16)
        sums = dot(lines, j_high[...], ((1,), (1,))) + dot(lines, j_low[...], ((1,), (1,)))
        return sums.reshape(4, 2, 4, 8, 640)

    part[...] = row_part(1 - core)
    across = exchange(part, got, partner)
    xr[...] = row_part(core)
    across.wait_recv()
    xr[...] += got[...]
    rows.step1()
    cols.step2()
    rows.step2()
    cols.step3()
    cols.step4()
    rows.step3()

    def line_weights(first):
        at = lax.broadcasted_iota(jnp.int32, (16, 512), 0)
        lane = lax.broadcasted_iota(jnp.int32, (16, 512), 1)
        at = jnp.where(at < 8, at, at + 24) + first
        return jnp.sum(jnp.where(lane == at, w_ref[...], 0.0), axis=1, keepdims=True)

    def residual(energy, hot, residue, weight):
        member = lax.broadcasted_iota(jnp.int32, (128, 640), 0) == residue
        member = member.astype(F32).astype(BF16)
        powers = jnp.exp(energy)
        lines = energy.shape[0]
        parts = dot(jnp.concatenate(three_parts(powers), axis=0), member, ((1,), (1,)))
        sums = parts[0:lines] + parts[lines : 2 * lines] + parts[2 * lines :]
        inverse = jnp.where(sums > 0.0, 1.0 / sums, 0.0)
        parts = dot(jnp.concatenate(three_parts(inverse), axis=0), member)
        inverse = parts[0:lines] + parts[lines : 2 * lines] + parts[2 * lines :]
        return weight * (powers * inverse - hot)

    energy = cols.result()
    column, second, valid = packed_column(lane_r)
    residue_c = jnp.where(valid, residue_of(column) + jnp.where(second, 32, 0), -1)
    first = x * 64 + z_lo * 8

    def column_lines(start):
        block = start // 8
        return jnp.concatenate([oc32[block], oc32[block + 4]], axis=0)

    hot1, hot2 = column_lines(first), column_lines(first + 256)
    hot = jnp.concatenate(
        [hot1[:, 0:256], hot2[:, 0:256], hot1[:, 256:384] + pltpu.roll(hot2[:, 256:384], 64, 1)],
        axis=1,
    )
    f_main, f_tail = states[8:16, 0:256], states[8:16, 256:384]
    fields_c = jnp.concatenate([f_main, f_main, f_tail + pltpu.roll(f_tail, 64, 1)], axis=1)[7:8]
    weight = jnp.where(second, line_weights(first + 256), line_weights(first))
    cols.gather1(residual(energy + fields_c, hot, residue_c, weight))
    rows.step4()
    cols.gather2()

    energy = rows.result()
    residue_rows = jnp.where(lane_r < 630, res_r, -1)
    block = core * 32 + y * 8 + z_hi
    hot = jnp.concatenate([or32[block], or32[block + 4]], axis=0)
    weight = line_weights(core * 256 + y * 64 + z_hi * 8)
    rows.gather1(residual(energy + fpad[0:1, :], hot, residue_rows, weight))
    cols.gather3()
    cols.gather4()
    rows.gather2()
    cols.gathered()

    def lines_of(source, first, lanes):
        return source[pl.ds(first, 32)].reshape(256, lanes).astype(BF16)

    whole = wc[...].reshape(256, 640)
    tail = whole[:, 512:640]
    tail_lane = lax.broadcasted_iota(jnp.int32, (1, 128), 1)
    tail1 = jnp.where(tail_lane < 64, tail, 0.0)
    tail2 = pltpu.roll(jnp.where(tail_lane < 64, 0.0, tail), 64, 1)
    first_c = jnp.concatenate([whole[:, 0:256], tail1], axis=1)
    second_c = jnp.concatenate([whole[:, 256:512], tail2], axis=1)
    total = None
    for n, lines in enumerate((first_c, second_c)):
        hot = lines_of(or32, 32 * n, 640)
        for piece in two_parts(lines):
            term = dot(hot, piece, ((0,), (0,)))
            total = term if total is None else total + term
    acc[...] = total

    rows.gather3()
    rows.gather4()

    last = []
    for h in range(2):
        own = wr.at[core, y, h]
        last.append(exchange(own, own, partner))
    for h in range(2):
        p, q = order(y, h)
        own = wr.at[core, q, h]
        last.append(exchange(own, own, partner))
    for h in range(2):
        p, q = order(y, h)
        for copy, i in zip(rows.g4[h], (p, far(y))):
            copy.wait_recv()
            own = wr.at[core, i, h]
            last.append(exchange(own, own, partner))

    def row_products(which):
        lines = wr[which].reshape(256, 640)
        hot = lines_of(oc32, which * 32, 384)
        high, low = two_parts(lines)
        sums = dot(high, hot, ((0,), (0,))) + dot(low, hot, ((0,), (0,)))
        return sums, jnp.sum(lines, axis=0, keepdims=True)

    sums, line_sum = row_products(core)
    acc[...] += sums
    for copy in last:
        copy.wait_recv()
    sums, other_sum = row_products(1 - core)
    fg_ref[...] = line_sum + other_sum
    total = acc[...] + sums
    g_ref[...] = total[0:630, 0:315]

    for copy in copies:
        copy.wait_send()

    @pl.when(row == owner)
    def _():
        for copy in state_copies:
            copy.wait_send()


def adam_update(values, first_moment, second_moment, gradient):
    first_new = 0.9 * first_moment + 0.1 * gradient
    second_new = 0.999 * second_moment + 0.001 * gradient * gradient
    change = (
        0.05 * (first_new / (1.0 - 0.9**10)) / (jnp.sqrt(second_new / (1.0 - 0.999**10)) + 1e-08)
    )
    return (values - change, first_new, second_new)


def on_device(
    alignment, seq_weight, couplings, pair_mean, pair_square, fields, field_mean, field_square
):
    vmem = pl.BlockSpec(memory_space=pltpu.VMEM)
    sums, field_sums = pl.pallas_call(
        kernel,
        out_shape=(
            jax.ShapeDtypeStruct(couplings.shape, F32),
            jax.ShapeDtypeStruct((1, 640), F32),
        ),
        in_specs=[vmem] * 4,
        out_specs=(vmem, vmem),
        scratch_shapes=[
            pltpu.VMEM((16, 512), F32),
            pltpu.VMEM((64, 8, 384), F32),
            pltpu.VMEM((64, 8, 640), F32),
            pltpu.VMEM((640, 384), BF16),
            pltpu.VMEM((640, 384), BF16),
        ]
        + [pltpu.VMEM((4, 2, 4, 8, 640), F32)] * 4
        + [
            pltpu.VMEM((2, 2, 4, 8, 640), F32),
            pltpu.VMEM((2, 4, 8, 640), F32),
            pltpu.VMEM((2, 2, 8, 640), F32),
            pltpu.VMEM((2, 8, 640), F32),
        ] * 2
        + [
            pltpu.VMEM((2, 4, 2, 4, 8, 640), F32),
            pltpu.VMEM((4, 2, 4, 8, 640), F32),
            pltpu.VMEM((640, 384), F32),
            pltpu.VMEM((8, 640), F32),
            pltpu.SemaphoreType.DMA((16,)),
            pltpu.SemaphoreType.DMA((72,)),
            pltpu.SemaphoreType.DMA((72,)),
        ],
        compiler_params=pltpu.CompilerParams(collective_id=0, has_side_effects=True),
    )(alignment, seq_weight.reshape(1, -1), couplings, fields.reshape(1, -1))
    row_residues = alignment.shape[1]
    column_residues = couplings.shape[1] // Q
    row_ids = (
        lax.axis_index("row") * row_residues
        + lax.broadcasted_iota(jnp.int32, (couplings.shape[0], 1), 0) // Q
    )
    column_ids = (
        lax.axis_index("col") * column_residues
        + lax.broadcasted_iota(jnp.int32, (1, couplings.shape[1]), 1) // Q
    )
    pair_grad = jnp.where(row_ids != column_ids, sums, 0.0) + 0.2 * (L - 1) * couplings
    field_grad = field_sums[0, : fields.shape[0]]
    new_pairs, new_pair_mean, new_pair_square = adam_update(
        couplings, pair_mean, pair_square, pair_grad
    )
    new_fields, new_field_mean, new_field_square = adam_update(
        fields, field_mean, field_square, field_grad
    )
    return (new_pairs, new_pair_mean, new_pair_square, new_fields, new_field_mean, new_field_square)


def solution(mesh):
    block = P("row", "col")
    in_specs = (P(None, "row"), P(), block, block, block, P("row"), P("row"), P("row"))
    out_specs = (block, block, block, P("row"), P("row"), P("row"))
    return jax.shard_map(
        on_device, mesh=mesh, in_specs=in_specs, out_specs=out_specs, check_vma=False
    )
```

```python
import jax
import jax.numpy as jnp
from jax import lax
from jax.experimental import pallas as pl
from jax.experimental.pallas import tpu as pltpu
from jax.sharding import PartitionSpec as P

L = 480
Q = 21
MESH = pl.DeviceIdType.MESH
F32 = jnp.float32
BF16 = jnp.bfloat16
ROW_GROUPS = ((0, 384), (384, 640))


def two_parts(x):
    high = x.astype(BF16)
    return high, (x - high.astype(F32)).astype(BF16)


def three_parts(x):
    high = x.astype(BF16)
    rest = x - high.astype(F32)
    mid = rest.astype(BF16)
    return high, mid, (rest - mid.astype(F32)).astype(BF16)


def dot(a, b, dims=((1,), (0,))):
    return lax.dot_general(a, b, (dims, ((), ())), preferred_element_type=F32)


def residue_of(lane):
    return ((lane.astype(F32) + 0.5) * (1.0 / Q)).astype(jnp.int32)


def flip(i):
    return i + 1 - 2 * (i % 2)


def mirror(i):
    return 3 - i


def packed_column(lane):
    main = jnp.where(lane < 256, lane, lane - 256)
    tail = jnp.where(lane < 576, lane - 512, lane - 576)
    column = jnp.where(lane < 512, main, tail + 256)
    second = ((lane >= 256) & (lane < 512)) | (lane >= 576)
    return column, second, (lane < 512) | (tail < 59)


def iota(shape, dim):
    return lax.broadcasted_iota(jnp.int32, shape, dim)


def as_bf16(mask):
    return mask.astype(F32).astype(BF16)


def order(i, half):
    first, second = flip(i), mirror(i)
    return (first, second) if half == 0 else (second, first)


def far(i):
    return (i + 2) % 4


class Reduce:
    def __init__(self, exchange, a, b, at, total, ins, full, groups):
        self.exchange, self.a, self.b, self.at = exchange, a, b, at
        self.total, self.ins, self.full, self.groups = total, ins, full, groups
        self.s1, self.s2, self.s3, self.s4 = {}, {}, {}, {}
        self.g1, self.g2, self.g3 = {}, {}, {}

    def lanes(self, g):
        low, high = self.groups[g]
        return pl.ds(low, high - low)

    def step1(self, g):
        at = self.lanes(g)
        for h in range(2):
            p, _ = order(self.a, h)
            to = self.at(p, self.b)
            later = self.total.at[far(self.a), h, :, :, at]
            theirs = self.total.at[p, h, :, :, at]
            one = self.exchange(later, self.ins[0].at[h, 1, :, :, at], to)
            two = self.exchange(theirs, self.ins[0].at[h, 0, :, :, at], to)
            self.s1[g, h] = (two, one)

    def step2(self, g):
        at = self.lanes(g)
        for h in range(2):
            p, q = order(self.a, h)
            self.s1[g, h][1].wait_recv()
            self.total[q, h, :, :, at] += self.ins[0][h, 1, :, :, at]
            self.s2[g, h] = self.exchange(
                self.total.at[q, h, :, :, at], self.ins[1].at[h, :, :, at], self.at(q, self.b)
            )
        for h in range(2):
            self.s1[g, h][0].wait_recv()
            self.total[self.a, h, :, :, at] += self.ins[0][h, 0, :, :, at]

    def step3(self, g):
        at = self.lanes(g)
        for h in range(2):
            p, _ = order(self.b, h)
            self.s2[g, h].wait_recv()
            self.total[self.a, h, :, :, at] += self.ins[1][h, :, :, at]
            to = self.at(self.a, p)
            self.s3[g, h] = [
                self.exchange(self.total.at[self.a, h, i, :, at], self.ins[2].at[h, n, :, at], to)
                for n, i in enumerate((p, far(self.b)))
            ]

    def step4(self, g):
        at = self.lanes(g)
        for h in range(2):
            p, q = order(self.b, h)
            to = self.at(self.a, q)
            for n, i in enumerate((self.b, q)):
                self.s3[g, h][n].wait_recv()
                self.total[self.a, h, i, :, at] += self.ins[2][h, n, :, at]
            self.s4[g, h] = [
                self.exchange(self.total.at[self.a, h, i, :, at], self.ins[3].at[h, 1 - n, :, at], to)
                for n, i in enumerate((self.b, q))
            ]

    def blocks(self):
        return [(h, i) for h in range(2) for i in (self.b, order(self.b, h)[1])]

    def result(self):
        for sent in self.s4.values():
            for copy in sent:
                copy.wait_recv()
        parts = [
            self.total[self.a, h, i] + self.ins[3][h, n % 2] for n, (h, i) in enumerate(self.blocks())
        ]
        return jnp.concatenate(parts, axis=0)

    def gather1(self, value):
        for n, (h, i) in enumerate(self.blocks()):
            self.full[self.a, h, i] = value[8 * n : 8 * n + 8]
        for g in range(len(self.groups)):
            at = self.lanes(g)
            for h in range(2):
                p, q = order(self.b, h)
                self.g1[g, h] = [
                    self.exchange(
                        self.full.at[self.a, h, i, :, at],
                        self.full.at[self.a, h, i, :, at],
                        self.at(self.a, p),
                    )
                    for i in (self.b, q)
                ]

    def gather2(self, g):
        at = self.lanes(g)
        for h in range(2):
            p, q = order(self.a, h)
            for copy in self.g1[g, h]:
                copy.wait_recv()
            own = self.full.at[self.a, h, :, :, at]
            self.g2[g, h] = self.exchange(own, own, self.at(q, self.b))
            self.g3[g, h] = [self.exchange(own, own, self.at(p, self.b))]

    def gather3(self, g):
        at = self.lanes(g)
        for h in range(2):
            p, q = order(self.a, h)
            second = self.full.at[q, h, :, :, at]
            self.g2[g, h].wait_recv()
            self.g3[g, h].append(self.exchange(second, second, self.at(p, self.b)))

    def gathered(self, g):
        for h in range(2):
            for copy in self.g3[g, h]:
                copy.wait_recv()


def kernel(
    al_ref, w_ref, j_ref, f_ref, g_ref, fg_ref,
    states, oc32, or32, oct, j_high, j_low, j_in, xr, xc,
    r_in1, r_in2, r_in3, r_in4, c_in1, c_in2, c_in3, c_in4, wr, wc, acc,
    fpad, state_send, send, recv,
):
    row, col = lax.axis_index("row"), lax.axis_index("col")
    z_lo, x = row // 4, row % 4
    y, z_hi, core = col // 8, (col // 2) % 4, col % 2
    owner = col // 2

    def at_row(a, b):
        return (row, a * 8 + b * 2 + core)

    def at_col(a, b):
        return (b * 4 + a, col)

    partner = (row, y * 8 + z_hi * 2 + 1 - core)

    barrier = pltpu.get_barrier_semaphore()
    greeted = [at_row(flip(y), z_hi), at_row(mirror(y), z_hi), at_row(y, flip(z_hi))]
    greeted += [at_row(y, mirror(z_hi)), partner]
    greeted += [((row + d) % 16, col) for d in range(1, 16)]
    for device in greeted:
        pl.semaphore_signal(barrier, inc=1, device_id=device, device_id_type=MESH)

    fpad[...] = jnp.zeros_like(fpad)
    fpad[0:1, 0:630] = f_ref[...]
    fields = fpad[...]
    field_lane = iota((8, 640), 1)
    fields0 = jnp.where(field_lane < 315, fields, 0.0)[0:1, 0:512]
    fields1 = jnp.where(field_lane < 315, pltpu.roll(fields, 325, 1), 0.0)[0:1, 0:512]
    alignment = al_ref[...].astype(F32).astype(BF16)
    word_row, word_residue = iota((8, 30), 0), iota((8, 30), 1)
    digit = word_residue - 5 * word_row
    scale = jnp.zeros((8, 30), F32)
    for d in range(5):
        scale = jnp.where(digit == d, float(Q**d), scale)
    words = sum(dot(part, alignment) for part in three_parts(scale))
    word_line = iota((8, 512), 0)
    words = jnp.where(word_line == 6, fields0, jnp.where(word_line == 7, fields1, words))

    pl.semaphore_wait(barrier, len(greeted))

    state_copies = [
        pltpu.make_async_remote_copy(
            states, states, state_send.at[d], recv.at[0],
            device_id=((row + d) % 16, col), device_id_type=MESH,
        )
        for d in range(1, 16)
    ]

    @pl.when(row == owner)
    def _():
        states[...] = words
        for copy in state_copies:
            copy.start()

    copies = []

    def exchange(src, dst, device):
        at = len(copies) + 1
        copy = pltpu.make_async_remote_copy(
            src, dst, send.at[at], recv.at[at], device_id=device, device_id_type=MESH
        )
        copy.start()
        copies.append(copy)
        return copy

    across = exchange(j_ref, j_in, partner)
    j_high[...] = jnp.zeros_like(j_high)
    j_low[...] = jnp.zeros_like(j_low)
    high, low = two_parts(j_ref[...])
    j_high[0:315, 0:630] = high
    j_low[0:315, 0:630] = low

    lane_r = iota((1, 640), 1)
    res_r = residue_of(lane_r)
    spread_r = iota((30, 640), 0) == residue_of(iota((30, 640), 1))
    value_r = dot(alignment, as_bf16(spread_r), ((0,), (0,)))
    hot_r = (value_r == (lane_r - res_r * Q).astype(F32)) & (lane_r < 630)
    hot_r = hot_r.astype(F32)
    or32[...] = hot_r.reshape(64, 8, 640)
    hot_r = hot_r.astype(BF16)

    nt = ((1,), (1,))
    top, bottom = hot_r[0:256], hot_r[256:512]
    none = jnp.zeros((64, 640), BF16)
    tails = [j[256:320] for j in (j_high, j_low)]
    tails1 = [jnp.concatenate([tail, none], axis=0) for tail in tails]
    tails2 = [jnp.concatenate([none, tail], axis=0) for tail in tails]
    mains = [j[0:256] for j in (j_high, j_low)]
    xc[:, :, :, :, 0:256] = sum(dot(top, j, nt) for j in mains).reshape(4, 2, 4, 8, 256)
    xc[:, :, :, :, 256:512] = sum(dot(bottom, j, nt) for j in mains).reshape(4, 2, 4, 8, 256)
    xc[:, :, :, :, 512:640] = (
        sum(dot(top, j, nt) for j in tails1) + sum(dot(bottom, j, nt) for j in tails2)
    ).reshape(4, 2, 4, 8, 128)

    cols = Reduce(
        exchange, x, z_lo, at_col, xc, (c_in1, c_in2, c_in3, c_in4), wc, ((0, 640),)
    )
    rows = Reduce(
        exchange, y, z_hi, at_row, xr, (r_in1, r_in2, r_in3, r_in4), wr.at[core], ROW_GROUPS
    )
    row_groups = range(len(ROW_GROUPS))
    cols.step1(0)

    across.wait_recv()
    high, low = two_parts(j_in[...])
    j_high[320:635, 0:630] = high
    j_low[320:635, 0:630] = low

    @pl.when(row != owner)
    def _():
        state_copies[0].wait_recv()

    rest = jnp.where(word_line < 6, states[...], 0.0)
    digits = []
    for _ in range(4):
        quotient = jnp.floor(rest * (1.0 / Q))
        remainder = rest - quotient * Q
        over, under = remainder >= Q, remainder < 0.0
        quotient = jnp.where(over, quotient + 1.0, jnp.where(under, quotient - 1.0, quotient))
        remainder = jnp.where(over, remainder - Q, jnp.where(under, remainder + Q, remainder))
        digits.append(remainder)
        rest = quotient
    digits = jnp.concatenate(digits + [rest], axis=0).astype(BF16)

    def digit_residue(shape, dim):
        at = iota(shape, dim)
        line = at % 8
        return jnp.where(line < 6, 5 * line + at // 8, -1)

    lane_b = iota((40, 640), 1)
    block_b = jnp.where(lane_b < 320, core, 1 - core)
    local_b = jnp.where(lane_b < 320, lane_b, lane_b - 320)
    spread_b = digit_residue((40, 640), 0) == block_b * 15 + residue_of(local_b)
    own_digits = jnp.where(core == 0, digits[:, 0:256].astype(F32), digits[:, 256:512].astype(F32))
    value_b = dot(own_digits.astype(BF16), as_bf16(spread_b), ((0,), (0,)))
    local = jnp.where(lane_r < 320, lane_r, lane_r - 320)
    hot_b = (value_b == (local - residue_of(local) * Q).astype(F32)) & (local < 315)
    hot_b = as_bf16(hot_b)
    for g in row_groups:
        at = rows.lanes(g)
        sums = dot(hot_b, j_high[:, at]) + dot(hot_b, j_low[:, at])
        xr[:, :, :, :, at] = sums.reshape(4, 2, 4, 8, -1)
        rows.step1(g)

    lane_c = iota((1, 384), 1)
    spread_c = digit_residue((40, 384), 0) == core * 15 + residue_of(iota((40, 384), 1))
    value_c = dot(digits, as_bf16(spread_c), ((0,), (0,)))
    hot_c = (value_c == (lane_c - residue_of(lane_c) * Q).astype(F32)) & (lane_c < 315)
    oc32[...] = hot_c.astype(F32).reshape(64, 8, 384)
    line_c = iota((320, 1), 0)
    spread_t = digit_residue((320, 40), 1) == core * 15 + residue_of(iota((320, 40), 0))
    value_t = dot(as_bf16(spread_t), digits)
    hot_t = (value_t == (line_c - residue_of(line_c) * Q).astype(F32)) & (line_c < 315)
    hot_t = as_bf16(hot_t)
    oct[0] = hot_t[:, 0:256]
    oct[1] = hot_t[:, 256:512]

    cols.step2(0)
    for g in row_groups:
        rows.step2(g)
    cols.step3(0)
    for g in row_groups:
        rows.step3(g)
    cols.step4(0)

    def line_weights(first):
        lane = iota((8, 512), 1) - iota((8, 512), 0)
        found = [jnp.where(lane == first + 32 * h + 8 * i, w_ref[...], 0.0) for h, i in first_blocks]
        return jnp.sum(jnp.concatenate(found, axis=0), axis=1, keepdims=True)

    def residual(energy, hot, residue, weight):
        member = as_bf16(iota((128, 640), 0) == residue)
        powers = jnp.exp(energy)
        lines = energy.shape[0]
        parts = dot(jnp.concatenate(three_parts(powers), axis=0), member, nt)
        sums = parts[0:lines] + parts[lines : 2 * lines] + parts[2 * lines :]
        inverse = jnp.where(sums > 0.0, 1.0 / sums, 0.0)
        parts = dot(jnp.concatenate(three_parts(inverse), axis=0), member)
        inverse = parts[0:lines] + parts[lines : 2 * lines] + parts[2 * lines :]
        return weight * (powers * inverse - hot)

    column, second, valid = packed_column(lane_r)
    residue_c = jnp.where(valid, residue_of(column) + jnp.where(second, 32, 0), -1)
    first = x * 64
    first_blocks = cols.blocks()

    def column_lines(start):
        return jnp.concatenate([oc32[start // 8 + 4 * h + i] for h, i in cols.blocks()], axis=0)

    hot1, hot2 = column_lines(first), column_lines(first + 256)
    hot = jnp.concatenate(
        [hot1[:, 0:256], hot2[:, 0:256], hot1[:, 256:384] + pltpu.roll(hot2[:, 256:384], 64, 1)],
        axis=1,
    )
    fields_c = jnp.where(core == 0, states[6:7, :], states[7:8, :])
    f_main, f_tail = fields_c[:, 0:256], jnp.broadcast_to(fields_c[:, 256:384], (8, 128))
    f_tail = (f_tail + pltpu.roll(f_tail, 64, 1))[0:1]
    fields_c = jnp.concatenate([f_main, f_main, f_tail], axis=1)
    weight = jnp.where(second, line_weights(first + 256), line_weights(first))
    cols.gather1(residual(cols.result() + fields_c, hot, residue_c, weight))
    for g in row_groups:
        rows.step4(g)
    cols.gather2(0)
    cols.gather3(0)

    residue_rows = jnp.where(lane_r < 630, res_r, -1)
    block = core * 32 + y * 8
    hot = jnp.concatenate([or32[block + 4 * h + i] for h, i in rows.blocks()], axis=0)
    first_blocks = rows.blocks()
    weight = line_weights(core * 256 + y * 64)
    rows.gather1(residual(rows.result() + fpad[0:1, :], hot, residue_rows, weight))

    cols.gathered(0)
    whole = wc[...].reshape(256, 640)
    tail = whole[:, 512:640]
    tail_lane = iota((1, 128), 1)
    tail1 = jnp.where(tail_lane < 64, tail, 0.0)
    tail2 = pltpu.roll(jnp.where(tail_lane < 64, 0.0, tail), 64, 1)
    first_c = jnp.concatenate([whole[:, 0:256], tail1], axis=1)
    second_c = jnp.concatenate([whole[:, 256:512], tail2], axis=1)

    def products(n, lines):
        hot = or32[32 * n : 32 * n + 32].reshape(256, 640).astype(BF16)
        return sum(dot(piece, hot, ((0,), (0,))) for piece in two_parts(lines))

    acc[...] = products(0, first_c) + products(1, second_c)

    for g in row_groups:
        rows.gather2(g)
    last = []

    def forward(i, h, g):
        piece = wr.at[core, i, h, :, :, rows.lanes(g)]
        last.append(exchange(piece, piece, partner))

    for g in row_groups:
        rows.gather3(g)
        for h in range(2):
            forward(y, h, g)
            forward(order(y, h)[1], h, g)
    for g in row_groups:
        rows.gathered(g)
        for h in range(2):
            forward(order(y, h)[0], h, g)
            forward(far(y), h, g)

    def row_products(which):
        lines = wr[which].reshape(256, 640)
        hot = oct[which]
        sums = sum(dot(hot, piece) for piece in two_parts(lines))
        return sums, jnp.sum(lines, axis=0, keepdims=True)

    sums, line_sum = row_products(core)
    acc[0:320, :] += sums
    for copy in last:
        copy.wait_recv()
    sums, other_sum = row_products(1 - core)
    fg_ref[...] = line_sum + other_sum
    total = acc[0:320, :] + sums
    g_ref[...] = total[0:315, 0:630]

    for copy in copies:
        copy.wait_send()

    @pl.when(row == owner)
    def _():
        for copy in state_copies:
            copy.wait_send()


def adam_update(values, first_moment, second_moment, gradient):
    first_new = 0.9 * first_moment + 0.1 * gradient
    second_new = 0.999 * second_moment + 0.001 * gradient * gradient
    change = (
        0.05 * (first_new / (1.0 - 0.9**10)) / (jnp.sqrt(second_new / (1.0 - 0.999**10)) + 1e-08)
    )
    return (values - change, first_new, second_new)


def on_device(
    alignment, seq_weight, couplings, pair_mean, pair_square, fields, field_mean, field_square
):
    vmem = pl.BlockSpec(memory_space=pltpu.VMEM)
    sums, field_sums = pl.pallas_call(
        kernel,
        out_shape=(
            jax.ShapeDtypeStruct(couplings.shape[::-1], F32),
            jax.ShapeDtypeStruct((1, 640), F32),
        ),
        in_specs=[vmem] * 4,
        out_specs=(vmem, vmem),
        scratch_shapes=[
            pltpu.VMEM((8, 512), F32),
            pltpu.VMEM((64, 8, 384), F32),
            pltpu.VMEM((64, 8, 640), F32),
            pltpu.VMEM((2, 320, 256), BF16),
            pltpu.VMEM((640, 640), BF16),
            pltpu.VMEM((640, 640), BF16),
            pltpu.VMEM(couplings.shape[::-1], F32),
        ]
        + [pltpu.VMEM((4, 2, 4, 8, 640), F32)] * 2
        + [
            pltpu.VMEM((2, 2, 4, 8, 640), F32),
            pltpu.VMEM((2, 4, 8, 640), F32),
            pltpu.VMEM((2, 2, 8, 640), F32),
            pltpu.VMEM((2, 2, 8, 640), F32),
        ] * 2
        + [
            pltpu.VMEM((2, 4, 2, 4, 8, 640), F32),
            pltpu.VMEM((4, 2, 4, 8, 640), F32),
            pltpu.VMEM((384, 640), F32),
            pltpu.VMEM((8, 640), F32),
            pltpu.SemaphoreType.DMA((16,)),
            pltpu.SemaphoreType.DMA((96,)),
            pltpu.SemaphoreType.DMA((96,)),
        ],
        compiler_params=pltpu.CompilerParams(collective_id=0, has_side_effects=True),
    )(alignment.T, seq_weight.reshape(1, -1), couplings.T, fields.reshape(1, -1))
    sums = sums.T
    row_residues = alignment.shape[1]
    column_residues = couplings.shape[1] // Q
    row_ids = (
        lax.axis_index("row") * row_residues
        + lax.broadcasted_iota(jnp.int32, (couplings.shape[0], 1), 0) // Q
    )
    column_ids = (
        lax.axis_index("col") * column_residues
        + lax.broadcasted_iota(jnp.int32, (1, couplings.shape[1]), 1) // Q
    )
    pair_grad = jnp.where(row_ids != column_ids, sums, 0.0) + 0.2 * (L - 1) * couplings
    field_grad = field_sums[0, : fields.shape[0]]
    new_pairs, new_pair_mean, new_pair_square = adam_update(
        couplings, pair_mean, pair_square, pair_grad
    )
    new_fields, new_field_mean, new_field_square = adam_update(
        fields, field_mean, field_square, field_grad
    )
    return (new_pairs, new_pair_mean, new_pair_square, new_fields, new_field_mean, new_field_square)


def solution(mesh):
    block = P("row", "col")
    in_specs = (P(None, "row"), P(), block, block, block, P("row"), P("row"), P("row"))
    out_specs = (block, block, block, P("row"), P("row"), P("row"))
    return jax.shard_map(
        on_device, mesh=mesh, in_specs=in_specs, out_specs=out_specs, check_vma=False
    )
```

```python
import jax
import jax.numpy as jnp
from jax import lax
from jax.experimental import pallas as pl
from jax.experimental.pallas import tpu as pltpu
from jax.sharding import PartitionSpec as P

L = 480
Q = 21
MESH = pl.DeviceIdType.MESH
F32 = jnp.float32
BF16 = jnp.bfloat16
VMEM_LIMIT = 24 * 2**20
ROW_GROUPS = ((0, 384), (384, 640))


def two_parts(x):
    high = x.astype(BF16)
    return high, (x - high.astype(F32)).astype(BF16)


def three_parts(x):
    high = x.astype(BF16)
    rest = x - high.astype(F32)
    mid = rest.astype(BF16)
    return high, mid, (rest - mid.astype(F32)).astype(BF16)


def dot(a, b, dims=((1,), (0,))):
    return lax.dot_general(a, b, (dims, ((), ())), preferred_element_type=F32)


def residue_of(lane):
    return ((lane.astype(F32) + 0.5) * (1.0 / Q)).astype(jnp.int32)


def flip(i):
    return i + 1 - 2 * (i % 2)


def mirror(i):
    return 3 - i


def packed_column(lane):
    main = jnp.where(lane < 256, lane, lane - 256)
    tail = jnp.where(lane < 576, lane - 512, lane - 576)
    column = jnp.where(lane < 512, main, tail + 256)
    second = ((lane >= 256) & (lane < 512)) | (lane >= 576)
    return column, second, (lane < 512) | (tail < 59)


def iota(shape, dim):
    return lax.broadcasted_iota(jnp.int32, shape, dim)


def as_bf16(mask):
    return mask.astype(F32).astype(BF16)


def order(i, half):
    first, second = flip(i), mirror(i)
    return (first, second) if half == 0 else (second, first)


def far(i):
    return (i + 2) % 4


class Reduce:
    def __init__(self, exchange, a, b, at, total, ins, full, groups):
        self.exchange, self.a, self.b, self.at = exchange, a, b, at
        self.total, self.ins, self.full, self.groups = total, ins, full, groups
        self.s1, self.s2, self.s3, self.s4 = {}, {}, {}, {}
        self.g1, self.g2, self.g3 = {}, {}, {}

    def lanes(self, g):
        low, high = self.groups[g]
        return pl.ds(low, high - low)

    def step1(self, g):
        at = self.lanes(g)
        for h in range(2):
            p, _ = order(self.a, h)
            to = self.at(p, self.b)
            later = self.total.at[far(self.a), h, :, :, at]
            theirs = self.total.at[p, h, :, :, at]
            one = self.exchange(later, self.ins[0].at[h, 1, :, :, at], to)
            two = self.exchange(theirs, self.ins[0].at[h, 0, :, :, at], to)
            self.s1[g, h] = (two, one)

    def step2(self, g):
        at = self.lanes(g)
        for h in range(2):
            p, q = order(self.a, h)
            self.s1[g, h][1].wait_recv()
            self.total[q, h, :, :, at] += self.ins[0][h, 1, :, :, at]
            self.s2[g, h] = self.exchange(
                self.total.at[q, h, :, :, at], self.ins[1].at[h, :, :, at], self.at(q, self.b)
            )
        for h in range(2):
            self.s1[g, h][0].wait_recv()
            self.total[self.a, h, :, :, at] += self.ins[0][h, 0, :, :, at]

    def step3(self, g):
        at = self.lanes(g)
        for h in range(2):
            p, _ = order(self.b, h)
            self.s2[g, h].wait_recv()
            self.total[self.a, h, :, :, at] += self.ins[1][h, :, :, at]
            to = self.at(self.a, p)
            self.s3[g, h] = [
                self.exchange(self.total.at[self.a, h, i, :, at], self.ins[2].at[h, n, :, at], to)
                for n, i in enumerate((p, far(self.b)))
            ]

    def step4(self, g):
        at = self.lanes(g)
        for h in range(2):
            p, q = order(self.b, h)
            to = self.at(self.a, q)
            for n, i in enumerate((self.b, q)):
                self.s3[g, h][n].wait_recv()
                self.total[self.a, h, i, :, at] += self.ins[2][h, n, :, at]
            self.s4[g, h] = [
                self.exchange(self.total.at[self.a, h, i, :, at], self.ins[3].at[h, 1 - n, :, at], to)
                for n, i in enumerate((self.b, q))
            ]

    def blocks(self):
        return [(h, i) for h in range(2) for i in (self.b, order(self.b, h)[1])]

    def result(self):
        for sent in self.s4.values():
            for copy in sent:
                copy.wait_recv()
        parts = [
            self.total[self.a, h, i] + self.ins[3][h, n % 2] for n, (h, i) in enumerate(self.blocks())
        ]
        return jnp.concatenate(parts, axis=0)

    def gather1(self, value):
        for n, (h, i) in enumerate(self.blocks()):
            self.full[self.a, h, i] = value[8 * n : 8 * n + 8]
        for g in range(len(self.groups)):
            at = self.lanes(g)
            for h in range(2):
                p, q = order(self.b, h)
                self.g1[g, h] = [
                    self.exchange(
                        self.full.at[self.a, h, i, :, at],
                        self.full.at[self.a, h, i, :, at],
                        self.at(self.a, p),
                    )
                    for i in (self.b, q)
                ]

    def gather2(self, g):
        at = self.lanes(g)
        for h in range(2):
            p, q = order(self.a, h)
            for copy in self.g1[g, h]:
                copy.wait_recv()
            own = self.full.at[self.a, h, :, :, at]
            self.g2[g, h] = self.exchange(own, own, self.at(q, self.b))
            self.g3[g, h] = [self.exchange(own, own, self.at(p, self.b))]

    def gather3(self, g):
        at = self.lanes(g)
        for h in range(2):
            p, q = order(self.a, h)
            second = self.full.at[q, h, :, :, at]
            self.g2[g, h].wait_recv()
            self.g3[g, h].append(self.exchange(second, second, self.at(p, self.b)))

    def gathered(self, g):
        for h in range(2):
            for copy in self.g3[g, h]:
                copy.wait_recv()


def kernel(
    al_in, w_in, j_ref, f_in, g_ref, fg_ref,
    states, oc32, or32, oct, j_high, j_low, j_in, xr, xc,
    r_in1, r_in2, r_in3, r_in4, c_in1, c_in2, c_in3, c_in4, wr, wc, acc,
    fpad, al_ref, w_ref, j_own, f_ref, local, state_send, send, recv,
):
    row, col = lax.axis_index("row"), lax.axis_index("col")
    z_lo, x = row // 4, row % 4
    y, z_hi, core = col // 8, (col // 2) % 4, col % 2
    owner = col // 2

    def at_row(a, b):
        return (row, a * 8 + b * 2 + core)

    def at_col(a, b):
        return (b * 4 + a, col)

    partner = (row, y * 8 + z_hi * 2 + 1 - core)

    barrier = pltpu.get_barrier_semaphore()
    greeted = [at_row(flip(y), z_hi), at_row(mirror(y), z_hi), at_row(y, flip(z_hi))]
    greeted += [at_row(y, mirror(z_hi)), partner]
    greeted += [((row + d) % 16, col) for d in range(1, 16)]
    for device in greeted:
        pl.semaphore_signal(barrier, inc=1, device_id=device, device_id_type=MESH)

    loads = [
        pltpu.make_async_copy(src, dst, local.at[n])
        for n, (src, dst) in enumerate(
            ((al_in, al_ref), (f_in, f_ref), (j_ref, j_own), (w_in, w_ref))
        )
    ]
    for load in loads:
        load.start()
    loads[0].wait()
    loads[1].wait()

    fpad[...] = jnp.zeros_like(fpad)
    fpad[0:1, 0:630] = f_ref[...].reshape(1, 630)
    fields = fpad[...]
    field_lane = iota((8, 640), 1)
    fields0 = jnp.where(field_lane < 315, fields, 0.0)[0:1, 0:512]
    fields1 = jnp.where(field_lane < 315, pltpu.roll(fields, 325, 1), 0.0)[0:1, 0:512]
    alignment = al_ref[...].astype(F32).astype(BF16)
    word_row, word_residue = iota((8, 30), 0), iota((8, 30), 1)
    digit = word_residue - 5 * word_row
    scale = jnp.zeros((8, 30), F32)
    for d in range(5):
        scale = jnp.where(digit == d, float(Q**d), scale)
    words = sum(dot(part, alignment) for part in three_parts(scale))
    word_line = iota((8, 512), 0)
    words = jnp.where(word_line == 6, fields0, jnp.where(word_line == 7, fields1, words))

    pl.semaphore_wait(barrier, len(greeted))

    state_copies = [
        pltpu.make_async_remote_copy(
            states, states, state_send.at[d], recv.at[0],
            device_id=((row + d) % 16, col), device_id_type=MESH,
        )
        for d in range(1, 16)
    ]

    @pl.when(row == owner)
    def _():
        states[...] = words
        for copy in state_copies:
            copy.start()

    copies = []

    def exchange(src, dst, device):
        at = len(copies) + 1
        copy = pltpu.make_async_remote_copy(
            src, dst, send.at[at], recv.at[at], device_id=device, device_id_type=MESH
        )
        copy.start()
        copies.append(copy)
        return copy

    across = exchange(j_ref, j_in, partner)
    j_high[...] = jnp.zeros_like(j_high)
    j_low[...] = jnp.zeros_like(j_low)
    loads[2].wait()
    loads[3].wait()
    high, low = two_parts(j_own[...])
    j_high[0:315, 0:630] = high
    j_low[0:315, 0:630] = low

    lane_r = iota((1, 640), 1)
    res_r = residue_of(lane_r)
    spread_r = iota((30, 640), 0) == residue_of(iota((30, 640), 1))
    value_r = dot(alignment, as_bf16(spread_r), ((0,), (0,)))
    hot_r = (value_r == (lane_r - res_r * Q).astype(F32)) & (lane_r < 630)
    hot_r = hot_r.astype(F32)
    or32[...] = hot_r.reshape(64, 8, 640)
    hot_r = hot_r.astype(BF16)

    nt = ((1,), (1,))
    top, bottom = hot_r[0:256], hot_r[256:512]
    none = jnp.zeros((64, 640), BF16)
    tails = [j[256:320] for j in (j_high, j_low)]
    tails1 = [jnp.concatenate([tail, none], axis=0) for tail in tails]
    tails2 = [jnp.concatenate([none, tail], axis=0) for tail in tails]
    mains = [j[0:256] for j in (j_high, j_low)]
    xc[:, :, :, :, 0:256] = sum(dot(top, j, nt) for j in mains).reshape(4, 2, 4, 8, 256)
    xc[:, :, :, :, 256:512] = sum(dot(bottom, j, nt) for j in mains).reshape(4, 2, 4, 8, 256)
    xc[:, :, :, :, 512:640] = (
        sum(dot(top, j, nt) for j in tails1) + sum(dot(bottom, j, nt) for j in tails2)
    ).reshape(4, 2, 4, 8, 128)

    cols = Reduce(
        exchange, x, z_lo, at_col, xc, (c_in1, c_in2, c_in3, c_in4), wc, ((0, 640),)
    )
    rows = Reduce(
        exchange, y, z_hi, at_row, xr, (r_in1, r_in2, r_in3, r_in4), wr.at[core], ROW_GROUPS
    )
    row_groups = range(len(ROW_GROUPS))
    cols.step1(0)

    across.wait_recv()
    high, low = two_parts(j_in[...])
    j_high[320:635, 0:630] = high
    j_low[320:635, 0:630] = low

    @pl.when(row != owner)
    def _():
        state_copies[0].wait_recv()

    rest = jnp.where(word_line < 6, states[...], 0.0)
    digits = []
    for _ in range(4):
        quotient = jnp.floor(rest * (1.0 / Q))
        remainder = rest - quotient * Q
        over, under = remainder >= Q, remainder < 0.0
        quotient = jnp.where(over, quotient + 1.0, jnp.where(under, quotient - 1.0, quotient))
        remainder = jnp.where(over, remainder - Q, jnp.where(under, remainder + Q, remainder))
        digits.append(remainder)
        rest = quotient
    digits = jnp.concatenate(digits + [rest], axis=0).astype(BF16)

    def digit_residue(shape, dim):
        at = iota(shape, dim)
        line = at % 8
        return jnp.where(line < 6, 5 * line + at // 8, -1)

    lane_b = iota((40, 640), 1)
    block_b = jnp.where(lane_b < 320, core, 1 - core)
    local_b = jnp.where(lane_b < 320, lane_b, lane_b - 320)
    spread_b = digit_residue((40, 640), 0) == block_b * 15 + residue_of(local_b)
    own_digits = jnp.where(core == 0, digits[:, 0:256].astype(F32), digits[:, 256:512].astype(F32))
    value_b = dot(own_digits.astype(BF16), as_bf16(spread_b), ((0,), (0,)))
    local = jnp.where(lane_r < 320, lane_r, lane_r - 320)
    hot_b = (value_b == (local - residue_of(local) * Q).astype(F32)) & (local < 315)
    hot_b = as_bf16(hot_b)
    for g in row_groups:
        at = rows.lanes(g)
        sums = dot(hot_b, j_high[:, at]) + dot(hot_b, j_low[:, at])
        xr[:, :, :, :, at] = sums.reshape(4, 2, 4, 8, -1)
        rows.step1(g)

    lane_c = iota((1, 384), 1)
    spread_c = digit_residue((40, 384), 0) == core * 15 + residue_of(iota((40, 384), 1))
    value_c = dot(digits, as_bf16(spread_c), ((0,), (0,)))
    hot_c = (value_c == (lane_c - residue_of(lane_c) * Q).astype(F32)) & (lane_c < 315)
    oc32[...] = hot_c.astype(F32).reshape(64, 8, 384)
    line_c = iota((320, 1), 0)
    spread_t = digit_residue((320, 40), 1) == core * 15 + residue_of(iota((320, 40), 0))
    value_t = dot(as_bf16(spread_t), digits)
    hot_t = (value_t == (line_c - residue_of(line_c) * Q).astype(F32)) & (line_c < 315)
    hot_t = as_bf16(hot_t)
    oct[0] = hot_t[:, 0:256]
    oct[1] = hot_t[:, 256:512]

    cols.step2(0)
    for g in row_groups:
        rows.step2(g)
    cols.step3(0)
    for g in row_groups:
        rows.step3(g)
    cols.step4(0)

    for g in row_groups:
        rows.step4(g)

    def line_weights(first):
        lane = iota((8, 512), 1) - iota((8, 512), 0)
        found = [jnp.where(lane == first + 32 * h + 8 * i, w_ref[...], 0.0) for h, i in first_blocks]
        return jnp.sum(jnp.concatenate(found, axis=0), axis=1, keepdims=True)

    def residual(energy, hot, residue, weight):
        member = as_bf16(iota((128, 640), 0) == residue)
        powers = jnp.exp(energy)
        lines = energy.shape[0]
        parts = dot(jnp.concatenate(three_parts(powers), axis=0), member, nt)
        sums = parts[0:lines] + parts[lines : 2 * lines] + parts[2 * lines :]
        inverse = jnp.where(sums > 0.0, 1.0 / sums, 0.0)
        parts = dot(jnp.concatenate(three_parts(inverse), axis=0), member)
        inverse = parts[0:lines] + parts[lines : 2 * lines] + parts[2 * lines :]
        return weight * (powers * inverse - hot)

    column, second, valid = packed_column(lane_r)
    residue_c = jnp.where(valid, residue_of(column) + jnp.where(second, 32, 0), -1)
    first = x * 64
    first_blocks = cols.blocks()

    def column_lines(start):
        return jnp.concatenate([oc32[start // 8 + 4 * h + i] for h, i in cols.blocks()], axis=0)

    hot1, hot2 = column_lines(first), column_lines(first + 256)
    hot = jnp.concatenate(
        [hot1[:, 0:256], hot2[:, 0:256], hot1[:, 256:384] + pltpu.roll(hot2[:, 256:384], 64, 1)],
        axis=1,
    )
    fields_c = jnp.where(core == 0, states[6:7, :], states[7:8, :])
    f_main, f_tail = fields_c[:, 0:256], jnp.broadcast_to(fields_c[:, 256:384], (8, 128))
    f_tail = (f_tail + pltpu.roll(f_tail, 64, 1))[0:1]
    fields_c = jnp.concatenate([f_main, f_main, f_tail], axis=1)
    weight = jnp.where(second, line_weights(first + 256), line_weights(first))
    cols.gather1(residual(cols.result() + fields_c, hot, residue_c, weight))
    cols.gather2(0)

    residue_rows = jnp.where(lane_r < 630, res_r, -1)
    block = core * 32 + y * 8
    hot = jnp.concatenate([or32[block + 4 * h + i] for h, i in rows.blocks()], axis=0)
    first_blocks = rows.blocks()
    weight = line_weights(core * 256 + y * 64)
    rows.gather1(residual(rows.result() + fpad[0:1, :], hot, residue_rows, weight))

    cols.gather3(0)
    for g in row_groups:
        rows.gather2(g)

    cols.gathered(0)
    whole = wc[...].reshape(256, 640)
    tail = whole[:, 512:640]
    tail_lane = iota((1, 128), 1)
    tail1 = jnp.where(tail_lane < 64, tail, 0.0)
    tail2 = pltpu.roll(jnp.where(tail_lane < 64, 0.0, tail), 64, 1)
    first_c = jnp.concatenate([whole[:, 0:256], tail1], axis=1)
    second_c = jnp.concatenate([whole[:, 256:512], tail2], axis=1)

    def products(n, lines):
        hot = or32[32 * n : 32 * n + 32].reshape(256, 640).astype(BF16)
        return sum(dot(piece, hot, ((0,), (0,))) for piece in two_parts(lines))

    acc[...] = products(0, first_c)
    last = []

    def forward(i, h, g):
        piece = wr.at[core, i, h, :, :, rows.lanes(g)]
        last.append(exchange(piece, piece, partner))

    for g in row_groups:
        rows.gather3(g)
        for h in range(2):
            forward(y, h, g)
            forward(order(y, h)[1], h, g)
    acc[...] += products(1, second_c)
    for g in row_groups:
        rows.gathered(g)
        for h in range(2):
            forward(order(y, h)[0], h, g)
            forward(far(y), h, g)

    def row_products(which):
        lines = wr[which].reshape(256, 640)
        hot = oct[which]
        sums = sum(dot(hot, piece) for piece in two_parts(lines))
        return sums, jnp.sum(lines, axis=0, keepdims=True)

    sums, line_sum = row_products(core)
    acc[0:320, :] += sums
    for copy in last:
        copy.wait_recv()
    sums, other_sum = row_products(1 - core)
    fg_ref[...] = line_sum + other_sum
    total = acc[0:320, :] + sums
    g_ref[...] = total[0:315, 0:630]

    for copy in copies:
        copy.wait_send()

    @pl.when(row == owner)
    def _():
        for copy in state_copies:
            copy.wait_send()


def adam_update(values, first_moment, second_moment, gradient):
    first_new = 0.9 * first_moment + 0.1 * gradient
    second_new = 0.999 * second_moment + 0.001 * gradient * gradient
    change = (
        0.05 * (first_new / (1.0 - 0.9**10)) / (jnp.sqrt(second_new / (1.0 - 0.999**10)) + 1e-08)
    )
    return (values - change, first_new, second_new)


def on_device(
    alignment, seq_weight, couplings, pair_mean, pair_square, fields, field_mean, field_square
):
    vmem = pl.BlockSpec(memory_space=pltpu.VMEM)
    sums, field_sums = pl.pallas_call(
        kernel,
        out_shape=(
            jax.ShapeDtypeStruct(couplings.shape[::-1], F32),
            jax.ShapeDtypeStruct((1, 640), F32),
        ),
        in_specs=[pl.BlockSpec(memory_space=pltpu.HBM)] * 4,
        out_specs=(vmem, vmem),
        scratch_shapes=[
            pltpu.VMEM((8, 512), F32),
            pltpu.VMEM((64, 8, 384), F32),
            pltpu.VMEM((64, 8, 640), F32),
            pltpu.VMEM((2, 320, 256), BF16),
            pltpu.VMEM((640, 640), BF16),
            pltpu.VMEM((640, 640), BF16),
            pltpu.VMEM(couplings.shape[::-1], F32),
        ]
        + [pltpu.VMEM((4, 2, 4, 8, 640), F32)] * 2
        + [
            pltpu.VMEM((2, 2, 4, 8, 640), F32),
            pltpu.VMEM((2, 4, 8, 640), F32),
            pltpu.VMEM((2, 2, 8, 640), F32),
            pltpu.VMEM((2, 2, 8, 640), F32),
        ] * 2
        + [
            pltpu.VMEM((2, 4, 2, 4, 8, 640), F32),
            pltpu.VMEM((4, 2, 4, 8, 640), F32),
            pltpu.VMEM((384, 640), F32),
            pltpu.VMEM((8, 640), F32),
            pltpu.VMEM(alignment.shape[::-1], jnp.int32),
            pltpu.VMEM((1, 512), F32),
            pltpu.VMEM(couplings.shape[::-1], F32),
            pltpu.VMEM(fields.shape, F32),
            pltpu.SemaphoreType.DMA((4,)),
            pltpu.SemaphoreType.DMA((16,)),
            pltpu.SemaphoreType.DMA((96,)),
            pltpu.SemaphoreType.DMA((96,)),
        ],
        compiler_params=pltpu.CompilerParams(collective_id=0, has_side_effects=True, vmem_limit_bytes=VMEM_LIMIT),
    )(*(
        pltpu.with_memory_space_constraint(x, pltpu.HBM)
        for x in (alignment.T, seq_weight.reshape(1, -1), couplings.T, fields)
    ))
    sums = sums.T
    row_residues = alignment.shape[1]
    column_residues = couplings.shape[1] // Q
    row_ids = (
        lax.axis_index("row") * row_residues
        + lax.broadcasted_iota(jnp.int32, (couplings.shape[0], 1), 0) // Q
    )
    column_ids = (
        lax.axis_index("col") * column_residues
        + lax.broadcasted_iota(jnp.int32, (1, couplings.shape[1]), 1) // Q
    )
    pair_grad = jnp.where(row_ids != column_ids, sums, 0.0) + 0.2 * (L - 1) * couplings
    field_grad = field_sums[0, : fields.shape[0]]
    new_pairs, new_pair_mean, new_pair_square = adam_update(
        couplings, pair_mean, pair_square, pair_grad
    )
    new_fields, new_field_mean, new_field_square = adam_update(
        fields, field_mean, field_square, field_grad
    )
    return (new_pairs, new_pair_mean, new_pair_square, new_fields, new_field_mean, new_field_square)


def solution(mesh):
    block = P("row", "col")
    in_specs = (P(None, "row"), P(), block, block, block, P("row"), P("row"), P("row"))
    out_specs = (block, block, block, P("row"), P("row"), P("row"))
    return jax.shard_map(
        on_device, mesh=mesh, in_specs=in_specs, out_specs=out_specs, check_vma=False
    )
```

```python
import jax
import jax.numpy as jnp
from jax import lax
from jax.experimental import pallas as pl
from jax.experimental.pallas import tpu as pltpu
from jax.sharding import PartitionSpec as P

L = 480
Q = 21
MESH = pl.DeviceIdType.MESH
F32 = jnp.float32
BF16 = jnp.bfloat16
VMEM_LIMIT = 24 * 2**20
ROW_GROUPS = ((0, 256), (256, 512), (512, 640))


def two_parts(x):
    high = x.astype(BF16)
    return high, (x - high.astype(F32)).astype(BF16)


def three_parts(x):
    high = x.astype(BF16)
    rest = x - high.astype(F32)
    mid = rest.astype(BF16)
    return high, mid, (rest - mid.astype(F32)).astype(BF16)


def dot(a, b, dims=((1,), (0,))):
    return lax.dot_general(a, b, (dims, ((), ())), preferred_element_type=F32)


def residue_of(lane):
    return ((lane.astype(F32) + 0.5) * (1.0 / Q)).astype(jnp.int32)


def flip(i):
    return i + 1 - 2 * (i % 2)


def mirror(i):
    return 3 - i


def packed_column(lane):
    main = jnp.where(lane < 256, lane, lane - 256)
    tail = jnp.where(lane < 576, lane - 512, lane - 576)
    column = jnp.where(lane < 512, main, tail + 256)
    second = ((lane >= 256) & (lane < 512)) | (lane >= 576)
    return column, second, (lane < 512) | (tail < 59)


def iota(shape, dim):
    return lax.broadcasted_iota(jnp.int32, shape, dim)


def as_bf16(mask):
    return mask.astype(F32).astype(BF16)


def order(i, half):
    first, second = flip(i), mirror(i)
    return (first, second) if half == 0 else (second, first)


def far(i):
    return (i + 2) % 4


def spread_lanes(x):
    at = iota((1, 128), 1)
    tiles = [x[:, 0:128]]
    for t in range(1, 5):
        last, this = x[:, 128 * t - 128 : 128 * t], x[:, 128 * t : 128 * t + 128]
        tiles.append(jnp.where(at < 2 * t, pltpu.roll(last, 2 * t, 1), pltpu.roll(this, 2 * t, 1)))
    return jnp.concatenate(tiles, axis=1)


def natural_tile(tile, t):
    at = iota((1, 128), 1)
    this = tile(t) if t == 0 else pltpu.roll(tile(t), 128 - 2 * t, 1)
    if t == 4:
        return this
    return jnp.where(at < 126 - 2 * t, this, pltpu.roll(tile(t + 1), 126 - 2 * t, 1))


class Reduce:
    def __init__(self, exchange, a, b, at, total, ins, full, groups):
        self.exchange, self.a, self.b, self.at = exchange, a, b, at
        self.total, self.ins, self.full, self.groups = total, ins, full, groups
        self.s1, self.s2, self.s3, self.s4 = {}, {}, {}, {}
        self.g1, self.g2, self.g3 = {}, {}, {}

    def lanes(self, g):
        low, high = self.groups[g]
        return pl.ds(low, high - low)

    def step1(self, g):
        at = self.lanes(g)
        for h in range(2):
            p, _ = order(self.a, h)
            to = self.at(p, self.b)
            later = self.total.at[far(self.a), h, :, :, at]
            theirs = self.total.at[p, h, :, :, at]
            one = self.exchange(later, self.ins[0].at[h, 1, :, :, at], to)
            two = self.exchange(theirs, self.ins[0].at[h, 0, :, :, at], to)
            self.s1[g, h] = (two, one)

    def step2(self, g):
        at = self.lanes(g)
        for h in range(2):
            p, q = order(self.a, h)
            self.s1[g, h][1].wait_recv()
            self.total[q, h, :, :, at] += self.ins[0][h, 1, :, :, at]
            self.s2[g, h] = self.exchange(
                self.total.at[q, h, :, :, at], self.ins[1].at[h, :, :, at], self.at(q, self.b)
            )
        for h in range(2):
            self.s1[g, h][0].wait_recv()
            self.total[self.a, h, :, :, at] += self.ins[0][h, 0, :, :, at]

    def step3(self, g):
        at = self.lanes(g)
        for h in range(2):
            p, _ = order(self.b, h)
            self.s2[g, h].wait_recv()
            self.total[self.a, h, :, :, at] += self.ins[1][h, :, :, at]
            to = self.at(self.a, p)
            self.s3[g, h] = [
                self.exchange(self.total.at[self.a, h, i, :, at], self.ins[2].at[h, n, :, at], to)
                for n, i in enumerate((p, far(self.b)))
            ]

    def step4(self, g):
        at = self.lanes(g)
        for h in range(2):
            p, q = order(self.b, h)
            to = self.at(self.a, q)
            for n, i in enumerate((self.b, q)):
                self.s3[g, h][n].wait_recv()
                self.total[self.a, h, i, :, at] += self.ins[2][h, n, :, at]
            self.s4[g, h] = [
                self.exchange(self.total.at[self.a, h, i, :, at], self.ins[3].at[h, 1 - n, :, at], to)
                for n, i in enumerate((self.b, q))
            ]

    def blocks(self):
        return [(h, i) for h in range(2) for i in (self.b, order(self.b, h)[1])]

    def result(self, g):
        at = self.lanes(g)
        for h in range(2):
            for copy in self.s4[g, h]:
                copy.wait_recv()
        parts = [
            self.total[self.a, h, i, :, at] + self.ins[3][h, n % 2, :, at]
            for n, (h, i) in enumerate(self.blocks())
        ]
        return jnp.concatenate(parts, axis=0)

    def gather1(self, g, value):
        at = self.lanes(g)
        for n, (h, i) in enumerate(self.blocks()):
            self.full[self.a, h, i, :, at] = value[8 * n : 8 * n + 8]
        for h in range(2):
            p, q = order(self.b, h)
            self.g1[g, h] = [
                self.exchange(
                    self.full.at[self.a, h, i, :, at],
                    self.full.at[self.a, h, i, :, at],
                    self.at(self.a, p),
                )
                for i in (self.b, q)
            ]

    def gather2(self, g):
        at = self.lanes(g)
        for h in range(2):
            p, q = order(self.a, h)
            for copy in self.g1[g, h]:
                copy.wait_recv()
            own = self.full.at[self.a, h, :, :, at]
            self.g2[g, h] = self.exchange(own, own, self.at(q, self.b))
            self.g3[g, h] = [self.exchange(own, own, self.at(p, self.b))]

    def gather3(self, g):
        at = self.lanes(g)
        for h in range(2):
            p, q = order(self.a, h)
            second = self.full.at[q, h, :, :, at]
            self.g2[g, h].wait_recv()
            self.g3[g, h].append(self.exchange(second, second, self.at(p, self.b)))

    def gathered(self, g):
        for h in range(2):
            for copy in self.g3[g, h]:
                copy.wait_recv()


def kernel(
    al_in, w_in, j_ref, f_in, fm_in, fs_in, g_ref, nf_ref, nfm_ref, nfs_ref,
    states, oc32, or32, oct, j_pad, j_high, j_low, j_in, xr, xc,
    r_in1, r_in2, r_in3, r_in4, c_in1, c_in2, c_in3, c_in4, wr, wc, acc,
    fpad, fg_ref, al_ref, w_ref, j_own, f_ref, fm_ref, fs_ref, local, state_send, send, recv,
):
    row, col = lax.axis_index("row"), lax.axis_index("col")
    z_lo, x = row // 4, row % 4
    y, z_hi, core = col // 8, (col // 2) % 4, col % 2
    owner = col // 2

    def at_row(a, b):
        return (row, a * 8 + b * 2 + core)

    def at_col(a, b):
        return (b * 4 + a, col)

    partner = (row, y * 8 + z_hi * 2 + 1 - core)

    barrier = pltpu.get_barrier_semaphore()
    greeted = [at_row(flip(y), z_hi), at_row(mirror(y), z_hi), at_row(y, flip(z_hi))]
    greeted += [at_row(y, mirror(z_hi)), partner]
    greeted += [((row + d) % 16, col) for d in range(1, 16)]
    for device in greeted:
        pl.semaphore_signal(barrier, inc=1, device_id=device, device_id_type=MESH)

    loads = [
        pltpu.make_async_copy(src, dst, local.at[n])
        for n, (src, dst) in enumerate(
            ((al_in, al_ref), (f_in, f_ref), (j_ref, j_own), (w_in, w_ref), (fm_in, fm_ref), (fs_in, fs_ref))
        )
    ]
    for load in loads:
        load.start()
    loads[0].wait()
    loads[1].wait()

    fpad[...] = jnp.zeros_like(fpad)
    fg_ref[...] = jnp.zeros_like(fg_ref)
    fpad[0:1, 0:630] = f_ref[...].reshape(1, 630)
    fields = fpad[...]
    field_lane = iota((8, 640), 1)
    fields0 = jnp.where(field_lane < 315, fields, 0.0)[0:1, 0:512]
    fields1 = jnp.where(field_lane < 315, pltpu.roll(fields, 325, 1), 0.0)[0:1, 0:512]
    alignment = al_ref[...].astype(F32).astype(BF16)
    word_row, word_residue = iota((8, 30), 0), iota((8, 30), 1)
    digit = word_residue - 5 * word_row
    scale = jnp.zeros((8, 30), F32)
    for d in range(5):
        scale = jnp.where(digit == d, float(Q**d), scale)
    words = sum(dot(part, alignment) for part in three_parts(scale))
    word_line = iota((8, 512), 0)
    words = jnp.where(word_line == 6, fields0, jnp.where(word_line == 7, fields1, words))

    loads[2].wait()
    for load in loads[3:]:
        load.wait()
    j_pad[...] = jnp.zeros_like(j_pad)
    j_pad[0:315, 0:630] = j_own[...]
    high, low = two_parts(spread_lanes(j_pad[...]))
    j_high[0:320, :] = high
    j_low[0:320, :] = low

    lane_r = iota((1, 640), 1)

    def tile_residue(lane):
        tile = lane // 128
        return tile * 6 + residue_of(lane - tile * 128)

    inside = lane_r % 128 < 126
    res_r = jnp.where(inside, tile_residue(lane_r), -1)
    state_r = (lane_r % 128) - residue_of(lane_r % 128) * Q
    spread_r = iota((30, 640), 0) == tile_residue(iota((30, 640), 1))
    value_r = dot(alignment, as_bf16(spread_r), ((0,), (0,)))
    hot_r = (value_r == state_r.astype(F32)) & inside
    hot_r = hot_r.astype(F32)
    or32[...] = hot_r.reshape(64, 8, 640)
    hot_r = hot_r.astype(BF16)

    pl.semaphore_wait(barrier, len(greeted))

    state_copies = [
        pltpu.make_async_remote_copy(
            states, states, state_send.at[d], recv.at[0],
            device_id=((row + d) % 16, col), device_id_type=MESH,
        )
        for d in range(1, 16)
    ]

    @pl.when(row == owner)
    def _():
        states[...] = words
        for copy in state_copies:
            copy.start()

    copies = []

    def exchange(src, dst, device):
        at = len(copies) + 1
        copy = pltpu.make_async_remote_copy(
            src, dst, send.at[at], recv.at[at], device_id=device, device_id_type=MESH
        )
        copy.start()
        copies.append(copy)
        return copy

    across = exchange(j_ref, j_in, partner)
    nt = ((1,), (1,))
    top, bottom = hot_r[0:256], hot_r[256:512]
    none = jnp.zeros((64, 640), BF16)
    tails = [j[256:320] for j in (j_high, j_low)]
    tails1 = [jnp.concatenate([tail, none], axis=0) for tail in tails]
    tails2 = [jnp.concatenate([none, tail], axis=0) for tail in tails]
    mains = [j[0:256] for j in (j_high, j_low)]
    xc[:, :, :, :, 0:256] = sum(dot(top, j, nt) for j in mains).reshape(4, 2, 4, 8, 256)
    xc[:, :, :, :, 256:512] = sum(dot(bottom, j, nt) for j in mains).reshape(4, 2, 4, 8, 256)
    xc[:, :, :, :, 512:640] = (
        sum(dot(top, j, nt) for j in tails1) + sum(dot(bottom, j, nt) for j in tails2)
    ).reshape(4, 2, 4, 8, 128)

    cols = Reduce(
        exchange, x, z_lo, at_col, xc, (c_in1, c_in2, c_in3, c_in4), wc, ((0, 640),)
    )
    rows = Reduce(
        exchange, y, z_hi, at_row, xr, (r_in1, r_in2, r_in3, r_in4), wr.at[core], ROW_GROUPS
    )
    row_groups = range(len(ROW_GROUPS))
    cols.step1(0)

    across.wait_recv()
    j_pad[0:315, 0:630] = j_in[...]
    high, low = two_parts(spread_lanes(j_pad[...]))
    j_high[320:640, :] = high
    j_low[320:640, :] = low

    @pl.when(row != owner)
    def _():
        state_copies[0].wait_recv()

    rest = jnp.where(word_line < 6, states[...], 0.0)
    digits = []
    for _ in range(4):
        quotient = jnp.floor(rest * (1.0 / Q))
        remainder = rest - quotient * Q
        over, under = remainder >= Q, remainder < 0.0
        quotient = jnp.where(over, quotient + 1.0, jnp.where(under, quotient - 1.0, quotient))
        remainder = jnp.where(over, remainder - Q, jnp.where(under, remainder + Q, remainder))
        digits.append(remainder)
        rest = quotient
    digits = jnp.concatenate(digits + [rest], axis=0).astype(BF16)

    def digit_residue(shape, dim):
        at = iota(shape, dim)
        line = at % 8
        return jnp.where(line < 6, 5 * line + at // 8, -1)

    lane_b = iota((40, 640), 1)
    block_b = jnp.where(lane_b < 320, core, 1 - core)
    local_b = jnp.where(lane_b < 320, lane_b, lane_b - 320)
    spread_b = digit_residue((40, 640), 0) == block_b * 15 + residue_of(local_b)
    own_digits = jnp.where(core == 0, digits[:, 0:256].astype(F32), digits[:, 256:512].astype(F32))
    value_b = dot(own_digits.astype(BF16), as_bf16(spread_b), ((0,), (0,)))
    local = jnp.where(lane_r < 320, lane_r, lane_r - 320)
    hot_b = (value_b == (local - residue_of(local) * Q).astype(F32)) & (local < 315)
    hot_b = as_bf16(hot_b)
    for g in row_groups:
        at = rows.lanes(g)
        sums = dot(hot_b, j_high[:, at]) + dot(hot_b, j_low[:, at])
        xr[:, :, :, :, at] = sums.reshape(4, 2, 4, 8, -1)
        rows.step1(g)

    lane_c = iota((1, 384), 1)
    spread_c = digit_residue((40, 384), 0) == core * 15 + residue_of(iota((40, 384), 1))
    value_c = dot(digits, as_bf16(spread_c), ((0,), (0,)))
    hot_c = (value_c == (lane_c - residue_of(lane_c) * Q).astype(F32)) & (lane_c < 315)
    oc32[...] = hot_c.astype(F32).reshape(64, 8, 384)
    line_c = iota((320, 1), 0)
    spread_t = digit_residue((320, 40), 1) == core * 15 + residue_of(iota((320, 40), 0))
    value_t = dot(as_bf16(spread_t), digits)
    hot_t = (value_t == (line_c - residue_of(line_c) * Q).astype(F32)) & (line_c < 315)
    hot_t = as_bf16(hot_t)
    oct[0] = hot_t[:, 0:256]
    oct[1] = hot_t[:, 256:512]

    cols.step2(0)
    for g in row_groups:
        rows.step2(g)
    cols.step3(0)
    for g in row_groups:
        rows.step3(g)
    cols.step4(0)

    for g in row_groups:
        rows.step4(g)

    def line_weights(first):
        lane = iota((8, 512), 1) - iota((8, 512), 0)
        found = [jnp.where(lane == first + 32 * h + 8 * i, w_ref[...], 0.0) for h, i in first_blocks]
        return jnp.sum(jnp.concatenate(found, axis=0), axis=1, keepdims=True)

    def residual(energy, hot, residue, weight):
        member = as_bf16(iota((128, energy.shape[1]), 0) == residue)
        powers = jnp.exp(energy)
        lines = energy.shape[0]
        parts = dot(jnp.concatenate(three_parts(powers), axis=0), member, nt)
        sums = parts[0:lines] + parts[lines : 2 * lines] + parts[2 * lines :]
        inverse = jnp.where(sums > 0.0, 1.0 / sums, 0.0)
        parts = dot(jnp.concatenate(three_parts(inverse), axis=0), member)
        inverse = parts[0:lines] + parts[lines : 2 * lines] + parts[2 * lines :]
        return weight * (powers * inverse - hot)

    column, second, valid = packed_column(lane_r)
    residue_c = jnp.where(valid, residue_of(column) + jnp.where(second, 32, 0), -1)
    first = x * 64
    first_blocks = cols.blocks()

    def column_lines(start):
        return jnp.concatenate([oc32[start // 8 + 4 * h + i] for h, i in cols.blocks()], axis=0)

    hot1, hot2 = column_lines(first), column_lines(first + 256)
    hot = jnp.concatenate(
        [hot1[:, 0:256], hot2[:, 0:256], hot1[:, 256:384] + pltpu.roll(hot2[:, 256:384], 64, 1)],
        axis=1,
    )
    fields_c = jnp.where(core == 0, states[6:7, :], states[7:8, :])
    f_main, f_tail = fields_c[:, 0:256], jnp.broadcast_to(fields_c[:, 256:384], (8, 128))
    f_tail = (f_tail + pltpu.roll(f_tail, 64, 1))[0:1]
    fields_c = jnp.concatenate([f_main, f_main, f_tail], axis=1)
    weight = jnp.where(second, line_weights(first + 256), line_weights(first))
    cols.gather1(0, residual(cols.result(0) + fields_c, hot, residue_c, weight))

    block = core * 32 + y * 8
    first_blocks = rows.blocks()
    weight = line_weights(core * 256 + y * 64)
    fields_r = spread_lanes(fpad[...])[0:1]
    for g in row_groups:
        low, high = ROW_GROUPS[g]
        at = rows.lanes(g)
        hot = jnp.concatenate([or32[block + 4 * h + i, :, at] for h, i in rows.blocks()], axis=0)
        energy = rows.result(g) + fields_r[:, low:high]
        rows.gather1(g, residual(energy, hot, res_r[:, low:high], weight))
        if g == 0:
            cols.gather2(0)
    cols.gather3(0)
    for g in row_groups:
        rows.gather2(g)

    cols.gathered(0)
    whole = wc[...].reshape(256, 640)
    tail = whole[:, 512:640]
    tail_lane = iota((1, 128), 1)
    tail1 = jnp.where(tail_lane < 64, tail, 0.0)
    tail2 = pltpu.roll(jnp.where(tail_lane < 64, 0.0, tail), 64, 1)
    first_c = jnp.concatenate([whole[:, 0:256], tail1], axis=1)
    second_c = jnp.concatenate([whole[:, 256:512], tail2], axis=1)

    def products(n, lines):
        hot = or32[32 * n : 32 * n + 32].reshape(256, 640).astype(BF16)
        return sum(dot(piece, hot, ((0,), (0,))) for piece in two_parts(lines))

    acc[...] = products(0, first_c)
    last = {g: [] for g in row_groups}

    def forward(i, h, g):
        piece = wr.at[core, i, h, :, :, rows.lanes(g)]
        last[g].append(exchange(piece, piece, partner))

    for g in row_groups:
        rows.gather3(g)
        for h in range(2):
            forward(y, h, g)
            forward(order(y, h)[1], h, g)
    acc[...] += products(1, second_c)
    for g in row_groups:
        rows.gathered(g)
        for h in range(2):
            forward(order(y, h)[0], h, g)
            forward(far(y), h, g)

    def row_products(which, g):
        lines = wr[which, :, :, :, :, rows.lanes(g)].reshape(256, -1)
        hot = oct[which]
        acc[0:320, rows.lanes(g)] += sum(dot(hot, piece) for piece in two_parts(lines))
        return jnp.sum(lines, axis=0, keepdims=True)

    def finish(t):
        high = min(128 * t + 128, 630)
        tile = natural_tile(lambda i: acc[0:320, 128 * i : 128 * i + 128], t)
        g_ref[:, 128 * t : high] = tile[0:315, 0 : high - 128 * t]

    line_sums = [row_products(core, g) for g in row_groups]
    done = 0
    for g in row_groups:
        for copy in last[g]:
            copy.wait_recv()
        fg_ref[0:1, rows.lanes(g)] = line_sums[g] + row_products(1 - core, g)
        ready = ROW_GROUPS[g][1] // 128
        for t in range(done, ready - (ready < 5)):
            finish(t)
        done = ready - 1

    def grad_tile(i):
        return fg_ref[:, 128 * i : 128 * i + 128]

    grad = jnp.concatenate([natural_tile(grad_tile, t) for t in range(5)], axis=1)[0:1, 0:630]
    moments = (f_ref, fm_ref, fs_ref)
    new = adam_update(*(ref[...].reshape(1, 630) for ref in moments), grad)
    for ref, value in zip((nf_ref, nfm_ref, nfs_ref), new):
        ref[...] = value.reshape(630)

    for copy in copies:
        copy.wait_send()

    @pl.when(row == owner)
    def _():
        for copy in state_copies:
            copy.wait_send()


def adam_update(values, first_moment, second_moment, gradient):
    first_new = 0.9 * first_moment + 0.1 * gradient
    second_new = 0.999 * second_moment + 0.001 * gradient * gradient
    root = jnp.sqrt(second_new * (1.0 / (1.0 - 0.999**10)))
    change = first_new * (0.05 / (1.0 - 0.9**10)) / (root + 1e-08)
    return (values - change, first_new, second_new)


def on_device(
    alignment, seq_weight, couplings, pair_mean, pair_square, fields, field_mean, field_square
):
    vmem = pl.BlockSpec(memory_space=pltpu.VMEM)
    sums, new_fields, new_field_mean, new_field_square = pl.pallas_call(
        kernel,
        out_shape=(
            jax.ShapeDtypeStruct(couplings.shape[::-1], F32),
            *[jax.ShapeDtypeStruct(fields.shape, F32)] * 3,
        ),
        in_specs=[pl.BlockSpec(memory_space=pltpu.HBM)] * 6,
        out_specs=(vmem,) * 4,
        scratch_shapes=[
            pltpu.VMEM((8, 512), F32),
            pltpu.VMEM((64, 8, 384), F32),
            pltpu.VMEM((64, 8, 640), F32),
            pltpu.VMEM((2, 320, 256), BF16),
            pltpu.VMEM((320, 640), F32),
            pltpu.VMEM((640, 640), BF16),
            pltpu.VMEM((640, 640), BF16),
            pltpu.VMEM(couplings.shape[::-1], F32),
        ]
        + [pltpu.VMEM((4, 2, 4, 8, 640), F32)] * 2
        + [
            pltpu.VMEM((2, 2, 4, 8, 640), F32),
            pltpu.VMEM((2, 4, 8, 640), F32),
            pltpu.VMEM((2, 2, 8, 640), F32),
            pltpu.VMEM((2, 2, 8, 640), F32),
        ] * 2
        + [
            pltpu.VMEM((2, 4, 2, 4, 8, 640), F32),
            pltpu.VMEM((4, 2, 4, 8, 640), F32),
            pltpu.VMEM((384, 640), F32),
            pltpu.VMEM((8, 640), F32),
            pltpu.VMEM((8, 640), F32),
            pltpu.VMEM(alignment.shape[::-1], jnp.int32),
            pltpu.VMEM((1, 512), F32),
            pltpu.VMEM(couplings.shape[::-1], F32),
            *[pltpu.VMEM(fields.shape, F32)] * 3,
            pltpu.SemaphoreType.DMA((6,)),
            pltpu.SemaphoreType.DMA((16,)),
            pltpu.SemaphoreType.DMA((136,)),
            pltpu.SemaphoreType.DMA((136,)),
        ],
        compiler_params=pltpu.CompilerParams(collective_id=0, has_side_effects=True, vmem_limit_bytes=VMEM_LIMIT),
    )(*(
        pltpu.with_memory_space_constraint(x, pltpu.HBM)
        for x in (alignment.T, seq_weight.reshape(1, -1), couplings.T, fields, field_mean, field_square)
    ))
    sums = sums.T
    row_residues = alignment.shape[1]
    column_residues = couplings.shape[1] // Q
    row_ids = (
        lax.axis_index("row") * row_residues
        + lax.broadcasted_iota(jnp.int32, (couplings.shape[0], 1), 0) // Q
    )
    column_ids = (
        lax.axis_index("col") * column_residues
        + lax.broadcasted_iota(jnp.int32, (1, couplings.shape[1]), 1) // Q
    )
    pair_grad = jnp.where(row_ids != column_ids, sums, 0.0) + 0.2 * (L - 1) * couplings
    new_pairs, new_pair_mean, new_pair_square = adam_update(
        couplings, pair_mean, pair_square, pair_grad
    )
    return (new_pairs, new_pair_mean, new_pair_square, new_fields, new_field_mean, new_field_square)


def solution(mesh):
    block = P("row", "col")
    in_specs = (P(None, "row"), P(), block, block, block, P("row"), P("row"), P("row"))
    out_specs = (block, block, block, P("row"), P("row"), P("row"))
    return jax.shard_map(
        on_device, mesh=mesh, in_specs=in_specs, out_specs=out_specs, check_vma=False
    )
```

```python
import jax
import jax.numpy as jnp
from jax import lax
from jax.experimental import pallas as pl
from jax.experimental.pallas import tpu as pltpu
from jax.sharding import PartitionSpec as P

L = 480
Q = 21
MESH = pl.DeviceIdType.MESH
F32 = jnp.float32
BF16 = jnp.bfloat16
VMEM_LIMIT = 24 * 2**20
SENDS = 40
ROW_GROUPS = ((0, 256), (256, 512), (512, 640))


def two_parts(x):
    high = x.astype(BF16)
    return high, (x - high.astype(F32)).astype(BF16)


def three_parts(x):
    high = x.astype(BF16)
    rest = x - high.astype(F32)
    mid = rest.astype(BF16)
    return high, mid, (rest - mid.astype(F32)).astype(BF16)


def dot(a, b, dims=((1,), (0,))):
    return lax.dot_general(a, b, (dims, ((), ())), preferred_element_type=F32)


def residue_of(lane):
    return ((lane.astype(F32) + 0.5) * (1.0 / Q)).astype(jnp.int32)


def flip(i):
    return i + 1 - 2 * (i % 2)


def mirror(i):
    return 3 - i


def packed_column(lane):
    main = jnp.where(lane < 256, lane, lane - 256)
    tail = jnp.where(lane < 576, lane - 512, lane - 576)
    column = jnp.where(lane < 512, main, tail + 256)
    second = ((lane >= 256) & (lane < 512)) | (lane >= 576)
    return column, second, (lane < 512) | (tail < 59)


def iota(shape, dim):
    return lax.broadcasted_iota(jnp.int32, shape, dim)


def as_bf16(mask):
    return mask.astype(F32).astype(BF16)


def order(i, half):
    first, second = flip(i), mirror(i)
    return (first, second) if half == 0 else (second, first)


def far(i):
    return (i + 2) % 4


def spread_lanes(x):
    at = iota((1, 128), 1)
    tiles = [x[:, 0:128]]
    for t in range(1, 5):
        last, this = x[:, 128 * t - 128 : 128 * t], x[:, 128 * t : 128 * t + 128]
        tiles.append(jnp.where(at < 2 * t, pltpu.roll(last, 2 * t, 1), pltpu.roll(this, 2 * t, 1)))
    return jnp.concatenate(tiles, axis=1)


def natural_tile(tile, t):
    at = iota((1, 128), 1)
    this = tile(t) if t == 0 else pltpu.roll(tile(t), 128 - 2 * t, 1)
    if t == 4:
        return this
    return jnp.where(at < 126 - 2 * t, this, pltpu.roll(tile(t + 1), 126 - 2 * t, 1))


class Reduce:
    def __init__(self, exchange, a, b, at, total, ins, full):
        self.exchange, self.a, self.b, self.at = exchange, a, b, at
        self.total, self.ins, self.full = total, ins, full
        self.s1, self.s2, self.s3, self.s4 = {}, {}, {}, {}
        self.g1, self.g2, self.g3 = {}, {}, {}

    def step1(self, g):
        for h in range(2):
            p, _ = order(self.a, h)
            to = self.at(p, self.b)
            later = self.total[g].at[far(self.a), h]
            theirs = self.total[g].at[p, h]
            one = self.exchange(later, self.ins[0][g].at[h, 1], to)
            two = self.exchange(theirs, self.ins[0][g].at[h, 0], to)
            self.s1[g, h] = (two, one)

    def step2(self, g):
        for h in range(2):
            p, q = order(self.a, h)
            self.s1[g, h][1].wait_recv()
            self.total[g][q, h] += self.ins[0][g][h, 1]
            self.s2[g, h] = self.exchange(
                self.total[g].at[q, h], self.ins[1][g].at[h], self.at(q, self.b)
            )
        for h in range(2):
            self.s1[g, h][0].wait_recv()
            self.total[g][self.a, h] += self.ins[0][g][h, 0]

    def step3(self, g):
        for h in range(2):
            p, _ = order(self.b, h)
            self.s2[g, h].wait_recv()
            self.total[g][self.a, h] += self.ins[1][g][h]
            to = self.at(self.a, p)
            self.s3[g, h] = [
                self.exchange(self.total[g].at[self.a, h, i], self.ins[2][g].at[h, n], to)
                for n, i in enumerate((p, far(self.b)))
            ]

    def step4(self, g):
        for h in range(2):
            p, q = order(self.b, h)
            to = self.at(self.a, q)
            for n, i in enumerate((self.b, q)):
                self.s3[g, h][n].wait_recv()
                self.total[g][self.a, h, i] += self.ins[2][g][h, n]
            self.s4[g, h] = [
                self.exchange(self.total[g].at[self.a, h, i], self.ins[3][g].at[h, 1 - n], to)
                for n, i in enumerate((self.b, q))
            ]

    def blocks(self):
        return [(h, i) for h in range(2) for i in (self.b, order(self.b, h)[1])]

    def result(self, g):
        for h in range(2):
            for copy in self.s4[g, h]:
                copy.wait_recv()
        parts = [
            self.total[g][self.a, h, i] + self.ins[3][g][h, n % 2]
            for n, (h, i) in enumerate(self.blocks())
        ]
        return jnp.concatenate(parts, axis=0)

    def gather1(self, g, value):
        for n, (h, i) in enumerate(self.blocks()):
            self.full[g][self.a, h, i] = value[8 * n : 8 * n + 8]
        for h in range(2):
            p, q = order(self.b, h)
            self.g1[g, h] = [
                self.exchange(
                    self.full[g].at[self.a, h, i],
                    self.full[g].at[self.a, h, i],
                    self.at(self.a, p),
                )
                for i in (self.b, q)
            ]

    def gather2(self, g):
        for h in range(2):
            p, q = order(self.a, h)
            for copy in self.g1[g, h]:
                copy.wait_recv()
            own = self.full[g].at[self.a, h]
            self.g2[g, h] = self.exchange(own, own, self.at(q, self.b))
            self.g3[g, h] = [self.exchange(own, own, self.at(p, self.b))]

    def gather3(self, g):
        for h in range(2):
            p, q = order(self.a, h)
            second = self.full[g].at[q, h]
            self.g2[g, h].wait_recv()
            self.g3[g, h].append(self.exchange(second, second, self.at(p, self.b)))

    def gathered(self, g):
        for h in range(2):
            for copy in self.g3[g, h]:
                copy.wait_recv()


def kernel(
    al_in, w_in, j_ref, f_in, fm_in, fs_in, g_ref, field_ref,
    states, oc32, or32, oct, j_pad, j_high, j_low, j_in, xr, xc,
    r_in1, r_in2, r_in3, r_in4, c_in1, c_in2, c_in3, c_in4, wr, wc, acc,
    fpad, fg_ref, al_ref, w_ref, j_own, f_ref, fm_ref, fs_ref, local, state_send, send, recv,
):
    row, col = lax.axis_index("row"), lax.axis_index("col")
    z_lo, x = row // 4, row % 4
    y, z_hi, core = col // 8, (col // 2) % 4, col % 2
    owner = col // 2

    def at_row(a, b):
        return (row, a * 8 + b * 2 + core)

    def at_col(a, b):
        return (b * 4 + a, col)

    partner = (row, y * 8 + z_hi * 2 + 1 - core)

    loads = [
        pltpu.make_async_copy(src, dst, local.at[n])
        for n, (src, dst) in enumerate(
            ((al_in, al_ref), (f_in, f_ref), (j_ref, j_own), (w_in, w_ref), (fm_in, fm_ref), (fs_in, fs_ref))
        )
    ]
    for load in loads:
        load.start()

    barrier = pltpu.get_barrier_semaphore()
    greeted = [at_row(flip(y), z_hi), at_row(mirror(y), z_hi), at_row(y, flip(z_hi))]
    greeted += [at_row(y, mirror(z_hi)), partner]
    greeted += [((row + d) % 16, col) for d in range(1, 16)]
    for device in greeted:
        pl.semaphore_signal(barrier, inc=1, device_id=device, device_id_type=MESH)

    loads[0].wait()
    loads[1].wait()

    fpad[...] = jnp.zeros_like(fpad)
    fg_ref[...] = jnp.zeros_like(fg_ref)
    fpad[0:1, 0:630] = f_ref[...].reshape(1, 630)
    fields = fpad[...]
    field_lane = iota((8, 640), 1)
    fields0 = jnp.where(field_lane < 315, fields, 0.0)[0:1, 0:512]
    fields1 = jnp.where(field_lane < 315, pltpu.roll(fields, 325, 1), 0.0)[0:1, 0:512]
    alignment = al_ref[...].astype(F32).astype(BF16)
    word_row, word_residue = iota((8, 30), 0), iota((8, 30), 1)
    digit = word_residue - 5 * word_row
    scale = jnp.zeros((8, 30), F32)
    for d in range(5):
        scale = jnp.where(digit == d, float(Q**d), scale)
    words = sum(dot(part, alignment) for part in three_parts(scale))
    word_line = iota((8, 512), 0)
    words = jnp.where(word_line == 6, fields0, jnp.where(word_line == 7, fields1, words))

    loads[2].wait()
    for load in loads[3:]:
        load.wait()
    j_pad[...] = jnp.zeros_like(j_pad)
    j_pad[0:315, 0:630] = j_own[...]
    high, low = two_parts(spread_lanes(j_pad[...]))
    j_high[0:320, :] = high
    j_low[0:320, :] = low

    lane_r = iota((1, 640), 1)

    def tile_residue(lane):
        tile = lane // 128
        return tile * 6 + residue_of(lane - tile * 128)

    inside = lane_r % 128 < 126
    res_r = jnp.where(inside, tile_residue(lane_r), -1)
    state_r = (lane_r % 128) - residue_of(lane_r % 128) * Q
    spread_r = iota((30, 640), 0) == tile_residue(iota((30, 640), 1))
    value_r = dot(alignment, as_bf16(spread_r), ((0,), (0,)))
    hot_r = (value_r == state_r.astype(F32)) & inside
    hot_r = hot_r.astype(F32)
    or32[...] = hot_r.reshape(64, 8, 640)
    hot_r = hot_r.astype(BF16)

    pl.semaphore_wait(barrier, len(greeted))

    state_copies = [
        pltpu.make_async_remote_copy(
            states, states, state_send.at[d], recv.at[0],
            device_id=((row + d) % 16, col), device_id_type=MESH,
        )
        for d in range(1, 16)
    ]

    @pl.when(row == owner)
    def _():
        states[...] = words
        for copy in state_copies:
            copy.start()

    copies = []

    def exchange(src, dst, device):
        at = len(copies)
        if at >= SENDS:
            copies[at - SENDS].wait_send()
        copy = pltpu.make_async_remote_copy(
            src, dst, send.at[at % SENDS], recv.at[at + 1], device_id=device, device_id_type=MESH
        )
        copy.start()
        copies.append(copy)
        return copy

    across = exchange(j_ref, j_in, partner)
    nt = ((1,), (1,))
    top, bottom = hot_r[0:256], hot_r[256:512]
    none = jnp.zeros((64, 640), BF16)
    tails = [j[256:320] for j in (j_high, j_low)]
    tails1 = [jnp.concatenate([tail, none], axis=0) for tail in tails]
    tails2 = [jnp.concatenate([none, tail], axis=0) for tail in tails]
    mains = [j[0:256] for j in (j_high, j_low)]
    xc[:, :, :, :, 0:256] = sum(dot(top, j, nt) for j in mains).reshape(4, 2, 4, 8, 256)
    xc[:, :, :, :, 256:512] = sum(dot(bottom, j, nt) for j in mains).reshape(4, 2, 4, 8, 256)
    xc[:, :, :, :, 512:640] = (
        sum(dot(top, j, nt) for j in tails1) + sum(dot(bottom, j, nt) for j in tails2)
    ).reshape(4, 2, 4, 8, 128)

    cols = Reduce(
        exchange, x, z_lo, at_col, [xc], ([c_in1], [c_in2], [c_in3], [c_in4]), [wc]
    )
    rows = Reduce(
        exchange, y, z_hi, at_row, xr, (r_in1, r_in2, r_in3, r_in4), [w.at[core] for w in wr]
    )
    row_groups = range(len(ROW_GROUPS))

    def lanes(g):
        return slice(*ROW_GROUPS[g])

    cols.step1(0)

    across.wait_recv()
    j_pad[0:315, 0:630] = j_in[...]
    high, low = two_parts(spread_lanes(j_pad[...]))
    j_high[320:640, :] = high
    j_low[320:640, :] = low

    @pl.when(row != owner)
    def _():
        state_copies[0].wait_recv()

    rest = jnp.where(word_line < 6, states[...], 0.0)
    digits = []
    for _ in range(4):
        quotient = jnp.floor(rest * (1.0 / Q))
        remainder = rest - quotient * Q
        over, under = remainder >= Q, remainder < 0.0
        quotient = jnp.where(over, quotient + 1.0, jnp.where(under, quotient - 1.0, quotient))
        remainder = jnp.where(over, remainder - Q, jnp.where(under, remainder + Q, remainder))
        digits.append(remainder)
        rest = quotient
    digits = jnp.concatenate(digits + [rest], axis=0).astype(BF16)

    def digit_residue(shape, dim):
        at = iota(shape, dim)
        line = at % 8
        return jnp.where(line < 6, 5 * line + at // 8, -1)

    lane_b = iota((40, 640), 1)
    block_b = jnp.where(lane_b < 320, core, 1 - core)
    local_b = jnp.where(lane_b < 320, lane_b, lane_b - 320)
    spread_b = digit_residue((40, 640), 0) == block_b * 15 + residue_of(local_b)
    own_digits = jnp.where(core == 0, digits[:, 0:256].astype(F32), digits[:, 256:512].astype(F32))
    value_b = dot(own_digits.astype(BF16), as_bf16(spread_b), ((0,), (0,)))
    local = jnp.where(lane_r < 320, lane_r, lane_r - 320)
    hot_b = (value_b == (local - residue_of(local) * Q).astype(F32)) & (local < 315)
    hot_b = as_bf16(hot_b)
    for g in row_groups:
        at = lanes(g)
        sums = dot(hot_b, j_high[:, at]) + dot(hot_b, j_low[:, at])
        xr[g][...] = sums.reshape(4, 2, 4, 8, -1)
        rows.step1(g)

    lane_c = iota((1, 384), 1)
    spread_c = digit_residue((40, 384), 0) == core * 15 + residue_of(iota((40, 384), 1))
    value_c = dot(digits, as_bf16(spread_c), ((0,), (0,)))
    hot_c = (value_c == (lane_c - residue_of(lane_c) * Q).astype(F32)) & (lane_c < 315)
    oc32[...] = hot_c.astype(F32).reshape(64, 8, 384)
    line_c = iota((320, 1), 0)
    spread_t = digit_residue((320, 40), 1) == core * 15 + residue_of(iota((320, 40), 0))
    value_t = dot(as_bf16(spread_t), digits)
    hot_t = (value_t == (line_c - residue_of(line_c) * Q).astype(F32)) & (line_c < 315)
    hot_t = as_bf16(hot_t)
    oct[0] = hot_t[:, 0:256]
    oct[1] = hot_t[:, 256:512]

    cols.step2(0)
    for g in row_groups:
        rows.step2(g)
    cols.step3(0)
    for g in row_groups:
        rows.step3(g)
    cols.step4(0)

    for g in row_groups:
        rows.step4(g)

    def line_weights(first):
        lane = iota((8, 512), 1) - iota((8, 512), 0)
        found = [jnp.where(lane == first + 32 * h + 8 * i, w_ref[...], 0.0) for h, i in first_blocks]
        return jnp.sum(jnp.concatenate(found, axis=0), axis=1, keepdims=True)

    def residual(energy, hot, residue, weight):
        member = as_bf16(iota((128, energy.shape[1]), 0) == residue)
        powers = jnp.exp(energy)
        lines = energy.shape[0]
        parts = dot(jnp.concatenate(three_parts(powers), axis=0), member, nt)
        sums = parts[0:lines] + parts[lines : 2 * lines] + parts[2 * lines :]
        inverse = jnp.where(sums > 0.0, 1.0 / sums, 0.0)
        parts = dot(jnp.concatenate(three_parts(inverse), axis=0), member)
        inverse = parts[0:lines] + parts[lines : 2 * lines] + parts[2 * lines :]
        return weight * (powers * inverse - hot)

    column, second, valid = packed_column(lane_r)
    residue_c = jnp.where(valid, residue_of(column) + jnp.where(second, 32, 0), -1)
    first = x * 64
    first_blocks = cols.blocks()

    def column_lines(start):
        return jnp.concatenate([oc32[start // 8 + 4 * h + i] for h, i in cols.blocks()], axis=0)

    hot1, hot2 = column_lines(first), column_lines(first + 256)
    hot = jnp.concatenate(
        [hot1[:, 0:256], hot2[:, 0:256], hot1[:, 256:384] + pltpu.roll(hot2[:, 256:384], 64, 1)],
        axis=1,
    )
    fields_c = jnp.where(core == 0, states[6:7, :], states[7:8, :])
    f_main, f_tail = fields_c[:, 0:256], jnp.broadcast_to(fields_c[:, 256:384], (8, 128))
    f_tail = (f_tail + pltpu.roll(f_tail, 64, 1))[0:1]
    fields_c = jnp.concatenate([f_main, f_main, f_tail], axis=1)
    weight = jnp.where(second, line_weights(first + 256), line_weights(first))
    cols.gather1(0, residual(cols.result(0) + fields_c, hot, residue_c, weight))

    block = core * 32 + y * 8
    first_blocks = rows.blocks()
    weight = line_weights(core * 256 + y * 64)
    fields_r = spread_lanes(fpad[...])[0:1]
    for g in row_groups:
        low, high = ROW_GROUPS[g]
        at = lanes(g)
        hot = jnp.concatenate([or32[block + 4 * h + i, :, at] for h, i in rows.blocks()], axis=0)
        energy = rows.result(g) + fields_r[:, low:high]
        rows.gather1(g, residual(energy, hot, res_r[:, low:high], weight))
        if g == 0:
            cols.gather2(0)
    cols.gather3(0)
    for g in row_groups:
        rows.gather2(g)

    cols.gathered(0)
    whole = wc[...].reshape(256, 640)
    tail = whole[:, 512:640]
    tail_lane = iota((1, 128), 1)
    tail1 = jnp.where(tail_lane < 64, tail, 0.0)
    tail2 = pltpu.roll(jnp.where(tail_lane < 64, 0.0, tail), 64, 1)
    first_c = jnp.concatenate([whole[:, 0:256], tail1], axis=1)
    second_c = jnp.concatenate([whole[:, 256:512], tail2], axis=1)

    def products(n, lines):
        hot = or32[32 * n : 32 * n + 32].reshape(256, 640).astype(BF16)
        return sum(dot(piece, hot, ((0,), (0,))) for piece in two_parts(lines))

    acc[...] = products(0, first_c)
    last = {g: [] for g in row_groups}

    def forward(i, h, g):
        piece = wr[g].at[core, i, h]
        last[g].append(exchange(piece, piece, partner))

    for g in row_groups:
        rows.gather3(g)
        for h in range(2):
            forward(y, h, g)
            forward(order(y, h)[1], h, g)
    acc[...] += products(1, second_c)
    for g in row_groups:
        rows.gathered(g)
        for h in range(2):
            forward(order(y, h)[0], h, g)
            forward(far(y), h, g)

    for n, ref in enumerate((f_ref, fm_ref, fs_ref)):
        field_ref[n : n + 1, 0:630] = ref[...].reshape(1, 630)

    def row_products(which, g):
        lines = wr[g][which].reshape(256, -1)
        hot = oct[which]
        acc[0:320, lanes(g)] += sum(dot(hot, piece) for piece in two_parts(lines))
        return jnp.sum(lines, axis=0, keepdims=True)

    def finish(t):
        high = min(128 * t + 128, 630)
        tile = natural_tile(lambda i: acc[0:320, 128 * i : 128 * i + 128], t)
        g_ref[:, 128 * t : high] = tile[0:315, 0 : high - 128 * t]

    line_sums = [row_products(core, g) for g in row_groups]
    done = 0
    for g in row_groups:
        for copy in last[g]:
            copy.wait_recv()
        fg_ref[0:1, lanes(g)] = line_sums[g] + row_products(1 - core, g)
        ready = ROW_GROUPS[g][1] // 128
        for t in range(done, ready - (ready < 5)):
            finish(t)
        done = ready - 1

    def grad_tile(i):
        return fg_ref[:, 128 * i : 128 * i + 128]

    grad = jnp.concatenate([natural_tile(grad_tile, t) for t in range(5)], axis=1)
    field_ref[3:4, :] = grad[0:1]

    for copy in copies[-SENDS:]:
        copy.wait_send()

    @pl.when(row == owner)
    def _():
        for copy in state_copies:
            copy.wait_send()


def adam_update(values, first_moment, second_moment, gradient):
    first_new = 0.9 * first_moment + 0.1 * gradient
    second_new = 0.999 * second_moment + 0.001 * gradient * gradient
    root = jnp.sqrt(second_new * (1.0 / (1.0 - 0.999**10)))
    change = first_new * (0.05 / (1.0 - 0.9**10)) / (root + 1e-08)
    return (values - change, first_new, second_new)


def on_device(
    alignment, seq_weight, couplings, pair_mean, pair_square, fields, field_mean, field_square
):
    vmem = pl.BlockSpec(memory_space=pltpu.VMEM)

    def by_group(*dims):
        return [pltpu.VMEM((*dims, high - low), F32) for low, high in ROW_GROUPS]

    sums, field_lines = pl.pallas_call(
        kernel,
        out_shape=(
            jax.ShapeDtypeStruct(couplings.shape[::-1], F32),
            jax.ShapeDtypeStruct((4, 640), F32),
        ),
        in_specs=[pl.BlockSpec(memory_space=pltpu.HBM)] * 6,
        out_specs=(vmem, vmem),
        scratch_shapes=[
            pltpu.VMEM((8, 512), F32),
            pltpu.VMEM((64, 8, 384), F32),
            pltpu.VMEM((64, 8, 640), F32),
            pltpu.VMEM((2, 320, 256), BF16),
            pltpu.VMEM((320, 640), F32),
            pltpu.VMEM((640, 640), BF16),
            pltpu.VMEM((640, 640), BF16),
            pltpu.VMEM(couplings.shape[::-1], F32),
        ]
        + [by_group(4, 2, 4, 8), pltpu.VMEM((4, 2, 4, 8, 640), F32)]
        + [by_group(2, 2, 4, 8), by_group(2, 4, 8), by_group(2, 2, 8), by_group(2, 2, 8)]
        + [
            pltpu.VMEM((2, 2, 4, 8, 640), F32),
            pltpu.VMEM((2, 4, 8, 640), F32),
            pltpu.VMEM((2, 2, 8, 640), F32),
            pltpu.VMEM((2, 2, 8, 640), F32),
            by_group(2, 4, 2, 4, 8),
            pltpu.VMEM((4, 2, 4, 8, 640), F32),
            pltpu.VMEM((384, 640), F32),
            pltpu.VMEM((8, 640), F32),
            pltpu.VMEM((8, 640), F32),
            pltpu.VMEM(alignment.shape[::-1], jnp.int32),
            pltpu.VMEM((1, 512), F32),
            pltpu.VMEM(couplings.shape[::-1], F32),
            *[pltpu.VMEM(fields.shape, F32)] * 3,
            pltpu.SemaphoreType.DMA((6,)),
            pltpu.SemaphoreType.DMA((16,)),
            pltpu.SemaphoreType.DMA((SENDS,)),
            pltpu.SemaphoreType.DMA((26 + 32 * len(ROW_GROUPS),)),
        ],
        compiler_params=pltpu.CompilerParams(collective_id=0, has_side_effects=True, vmem_limit_bytes=VMEM_LIMIT),
    )(*(
        pltpu.with_memory_space_constraint(x, pltpu.HBM)
        for x in (alignment.T, seq_weight.reshape(1, -1), couplings.T, fields, field_mean, field_square)
    ))
    sums = sums.T
    row_residues = alignment.shape[1]
    column_residues = couplings.shape[1] // Q
    row_ids = (
        lax.axis_index("row") * row_residues
        + lax.broadcasted_iota(jnp.int32, (couplings.shape[0], 1), 0) // Q
    )
    column_ids = (
        lax.axis_index("col") * column_residues
        + lax.broadcasted_iota(jnp.int32, (1, couplings.shape[1]), 1) // Q
    )
    pair_grad = jnp.where(row_ids != column_ids, sums, 0.0) + 0.2 * (L - 1) * couplings
    new_pairs, new_pair_mean, new_pair_square = adam_update(
        couplings, pair_mean, pair_square, pair_grad
    )
    new_fields, new_field_mean, new_field_square = adam_update(
        *(field_lines[n, : fields.shape[0]] for n in range(4))
    )
    return (new_pairs, new_pair_mean, new_pair_square, new_fields, new_field_mean, new_field_square)


def solution(mesh):
    block = P("row", "col")
    in_specs = (P(None, "row"), P(), block, block, block, P("row"), P("row"), P("row"))
    out_specs = (block, block, block, P("row"), P("row"), P("row"))
    return jax.shard_map(
        on_device, mesh=mesh, in_specs=in_specs, out_specs=out_specs, check_vma=False
    )
```

```python
import jax
import jax.numpy as jnp
from jax import lax
from jax.experimental import pallas as pl
from jax.experimental.pallas import tpu as pltpu
from jax.sharding import PartitionSpec as P

L = 480
Q = 21
MESH = pl.DeviceIdType.MESH
F32 = jnp.float32
BF16 = jnp.bfloat16
VMEM_LIMIT = 24 * 2**20
SENDS = 40
ROW_GROUPS = ((0, 384), (384, 640))


def two_parts(x):
    high = x.astype(BF16)
    return high, (x - high.astype(F32)).astype(BF16)


def three_parts(x):
    high = x.astype(BF16)
    rest = x - high.astype(F32)
    mid = rest.astype(BF16)
    return high, mid, (rest - mid.astype(F32)).astype(BF16)


def dot(a, b, dims=((1,), (0,))):
    return lax.dot_general(a, b, (dims, ((), ())), preferred_element_type=F32)


def residue_of(lane):
    return ((lane.astype(F32) + 0.5) * (1.0 / Q)).astype(jnp.int32)


def flip(i):
    return i + 1 - 2 * (i % 2)


def mirror(i):
    return 3 - i


def packed_column(lane):
    main = jnp.where(lane < 256, lane, lane - 256)
    tail = jnp.where(lane < 576, lane - 512, lane - 576)
    column = jnp.where(lane < 512, main, tail + 256)
    second = ((lane >= 256) & (lane < 512)) | (lane >= 576)
    return column, second, (lane < 512) | (tail < 59)


def iota(shape, dim):
    return lax.broadcasted_iota(jnp.int32, shape, dim)


def as_bf16(mask):
    return mask.astype(F32).astype(BF16)


def order(i, half):
    first, second = flip(i), mirror(i)
    return (first, second) if half == 0 else (second, first)


def far(i):
    return (i + 2) % 4


def spread_lanes(x):
    at = iota((1, 128), 1)
    tiles = [x[:, 0:128]]
    for t in range(1, 5):
        last, this = x[:, 128 * t - 128 : 128 * t], x[:, 128 * t : 128 * t + 128]
        tiles.append(jnp.where(at < 2 * t, pltpu.roll(last, 2 * t, 1), pltpu.roll(this, 2 * t, 1)))
    return jnp.concatenate(tiles, axis=1)


def natural_tile(tile, t):
    at = iota((1, 128), 1)
    this = tile(t) if t == 0 else pltpu.roll(tile(t), 128 - 2 * t, 1)
    if t == 4:
        return this
    return jnp.where(at < 126 - 2 * t, this, pltpu.roll(tile(t + 1), 126 - 2 * t, 1))


class Reduce:
    def __init__(self, exchange, a, b, at, total, ins, full):
        self.exchange, self.a, self.b, self.at = exchange, a, b, at
        self.total, self.ins, self.full = total, ins, full
        self.s1, self.s2, self.s3, self.s4 = {}, {}, {}, {}
        self.g1, self.g2, self.g3 = {}, {}, {}

    def step1(self, g):
        for h in range(2):
            p, _ = order(self.a, h)
            to = self.at(p, self.b)
            later = self.total[g].at[far(self.a), h]
            theirs = self.total[g].at[p, h]
            one = self.exchange(later, self.ins[0][g].at[h, 1], to)
            two = self.exchange(theirs, self.ins[0][g].at[h, 0], to)
            self.s1[g, h] = (two, one)

    def step2(self, g):
        for h in range(2):
            p, q = order(self.a, h)
            self.s1[g, h][1].wait_recv()
            self.total[g][q, h] += self.ins[0][g][h, 1]
            self.s2[g, h] = self.exchange(
                self.total[g].at[q, h], self.ins[1][g].at[h], self.at(q, self.b)
            )
        for h in range(2):
            self.s1[g, h][0].wait_recv()
            self.total[g][self.a, h] += self.ins[0][g][h, 0]

    def pair(self, h, i):
        at = (i + 1) % 4 if h == 0 else i
        return at - at % 2

    def step3(self, g):
        for h in range(2):
            p, _ = order(self.b, h)
            self.s2[g, h].wait_recv()
            self.total[g][self.a, h] += self.ins[1][g][h]
            theirs = self.total[g].at[self.a, h, pl.ds(self.pair(h, p), 2)]
            self.s3[g, h] = self.exchange(theirs, self.ins[2][g].at[h], self.at(self.a, p))

    def step4(self, g):
        for h in range(2):
            _, q = order(self.b, h)
            mine = pl.ds(self.pair(h, self.b), 2)
            self.s3[g, h].wait_recv()
            self.total[g][self.a, h, mine] += self.ins[2][g][h]
            self.s4[g, h] = self.exchange(
                self.total[g].at[self.a, h, mine], self.ins[3][g].at[h], self.at(self.a, q)
            )

    def blocks(self):
        return [(h, self.pair(h, self.b) + n) for h in range(2) for n in range(2)]

    def result(self, g):
        for h in range(2):
            self.s4[g, h].wait_recv()
        parts = [
            self.total[g][self.a, h, i] + self.ins[3][g][h, n % 2]
            for n, (h, i) in enumerate(self.blocks())
        ]
        return jnp.concatenate(parts, axis=0)

    def gather1(self, g, value):
        for n, (h, i) in enumerate(self.blocks()):
            self.full[g][self.a, h, i] = value[8 * n : 8 * n + 8]
        for h in range(2):
            p, _ = order(self.b, h)
            mine = self.full[g].at[self.a, h, pl.ds(self.pair(h, self.b), 2)]
            self.g1[g, h] = self.exchange(mine, mine, self.at(self.a, p))

    def gather2(self, g):
        for h in range(2):
            p, q = order(self.a, h)
            self.g1[g, h].wait_recv()
            own = self.full[g].at[self.a, h]
            self.g2[g, h] = self.exchange(own, own, self.at(q, self.b))
            self.g3[g, h] = [self.exchange(own, own, self.at(p, self.b))]

    def gather3(self, g):
        for h in range(2):
            p, q = order(self.a, h)
            second = self.full[g].at[q, h]
            self.g2[g, h].wait_recv()
            self.g3[g, h].append(self.exchange(second, second, self.at(p, self.b)))

    def gathered(self, g):
        for h in range(2):
            for copy in self.g3[g, h]:
                copy.wait_recv()


def kernel(
    al_in, w_in, j_ref, f_in, fm_in, fs_in, pm_in, ps_in, g_ref, field_ref, pm_ref, ps_ref,
    states, oc32, or32, oct, j_pad, j_high, j_low, j_in, xr, xc,
    r_in1, r_in2, r_in3, r_in4, c_in1, c_in2, c_in3, c_in4, wr, wc, acc,
    fpad, fg_ref, al_ref, w_ref, j_own, f_ref, fm_ref, fs_ref, local, state_send, send, recv,
):
    row, col = lax.axis_index("row"), lax.axis_index("col")
    z_lo, x = row // 4, row % 4
    y, z_hi, core = col // 8, (col // 2) % 4, col % 2
    owner = col // 2

    def at_row(a, b):
        return (row, a * 8 + b * 2 + core)

    def at_col(a, b):
        return (b * 4 + a, col)

    partner = (row, y * 8 + z_hi * 2 + 1 - core)

    loads = [
        pltpu.make_async_copy(src, dst, local.at[n])
        for n, (src, dst) in enumerate(
            ((al_in, al_ref), (f_in, f_ref), (j_ref, j_own), (w_in, w_ref), (fm_in, fm_ref), (fs_in, fs_ref), (pm_in, pm_ref), (ps_in, ps_ref))
        )
    ]
    for load in loads:
        load.start()

    barrier = pltpu.get_barrier_semaphore()
    greeted = [at_row(flip(y), z_hi), at_row(mirror(y), z_hi), at_row(y, flip(z_hi))]
    greeted += [at_row(y, mirror(z_hi)), partner]
    greeted += [((row + d) % 16, col) for d in range(1, 16)]
    for device in greeted:
        pl.semaphore_signal(barrier, inc=1, device_id=device, device_id_type=MESH)

    loads[0].wait()
    loads[1].wait()

    fpad[...] = jnp.zeros_like(fpad)
    fg_ref[...] = jnp.zeros_like(fg_ref)
    fpad[0:1, 0:630] = f_ref[...].reshape(1, 630)
    fields = fpad[...]
    field_lane = iota((8, 640), 1)
    fields0 = jnp.where(field_lane < 315, fields, 0.0)[0:1, 0:512]
    fields1 = jnp.where(field_lane < 315, pltpu.roll(fields, 325, 1), 0.0)[0:1, 0:512]
    alignment = al_ref[...].astype(F32).astype(BF16)
    word_row, word_residue = iota((8, 30), 0), iota((8, 30), 1)
    digit = word_residue - 5 * word_row
    scale = jnp.zeros((8, 30), F32)
    for d in range(5):
        scale = jnp.where(digit == d, float(Q**d), scale)
    words = sum(dot(part, alignment) for part in three_parts(scale))
    word_line = iota((8, 512), 0)
    words = jnp.where(word_line == 6, fields0, jnp.where(word_line == 7, fields1, words))

    loads[2].wait()
    for load in loads[3:6]:
        load.wait()
    j_pad[...] = jnp.zeros_like(j_pad)
    j_pad[0:315, 0:630] = j_own[...]
    high, low = two_parts(spread_lanes(j_pad[...]))
    j_high[0:320, :] = high
    j_low[0:320, :] = low

    lane_r = iota((1, 640), 1)

    def tile_residue(lane):
        tile = lane // 128
        return tile * 6 + residue_of(lane - tile * 128)

    inside = lane_r % 128 < 126
    res_r = jnp.where(inside, tile_residue(lane_r), -1)
    state_r = (lane_r % 128) - residue_of(lane_r % 128) * Q
    spread_r = iota((30, 640), 0) == tile_residue(iota((30, 640), 1))
    value_r = dot(alignment, as_bf16(spread_r), ((0,), (0,)))
    hot_r = (value_r == state_r.astype(F32)) & inside
    hot_r = hot_r.astype(F32)
    or32[...] = hot_r.reshape(64, 8, 640)
    hot_r = hot_r.astype(BF16)

    pl.semaphore_wait(barrier, len(greeted))

    state_copies = [
        pltpu.make_async_remote_copy(
            states, states, state_send.at[d], recv.at[0],
            device_id=((row + d) % 16, col), device_id_type=MESH,
        )
        for d in range(1, 16)
    ]

    @pl.when(row == owner)
    def _():
        states[...] = words
        for copy in state_copies:
            copy.start()

    copies = []

    def exchange(src, dst, device):
        at = len(copies)
        if at >= SENDS:
            copies[at - SENDS].wait_send()
        copy = pltpu.make_async_remote_copy(
            src, dst, send.at[at % SENDS], recv.at[at + 1], device_id=device, device_id_type=MESH
        )
        copy.start()
        copies.append(copy)
        return copy

    across = exchange(j_ref, j_in, partner)
    nt = ((1,), (1,))
    top, bottom = hot_r[0:256], hot_r[256:512]
    none = jnp.zeros((64, 640), BF16)
    tails = [j[256:320] for j in (j_high, j_low)]
    tails1 = [jnp.concatenate([tail, none], axis=0) for tail in tails]
    tails2 = [jnp.concatenate([none, tail], axis=0) for tail in tails]
    mains = [j[0:256] for j in (j_high, j_low)]
    xc[:, :, :, :, 0:256] = sum(dot(top, j, nt) for j in mains).reshape(4, 2, 4, 8, 256)
    xc[:, :, :, :, 256:512] = sum(dot(bottom, j, nt) for j in mains).reshape(4, 2, 4, 8, 256)
    xc[:, :, :, :, 512:640] = (
        sum(dot(top, j, nt) for j in tails1) + sum(dot(bottom, j, nt) for j in tails2)
    ).reshape(4, 2, 4, 8, 128)

    cols = Reduce(
        exchange, x, z_lo, at_col, [xc], ([c_in1], [c_in2], [c_in3], [c_in4]), [wc]
    )
    rows = Reduce(
        exchange, y, z_hi, at_row, xr, (r_in1, r_in2, r_in3, r_in4), [w.at[core] for w in wr]
    )
    row_groups = range(len(ROW_GROUPS))

    def lanes(g):
        return slice(*ROW_GROUPS[g])

    cols.step1(0)

    across.wait_recv()
    j_pad[0:315, 0:630] = j_in[...]
    high, low = two_parts(spread_lanes(j_pad[...]))
    j_high[320:640, :] = high
    j_low[320:640, :] = low

    @pl.when(row != owner)
    def _():
        state_copies[0].wait_recv()

    rest = jnp.where(word_line < 6, states[...], 0.0)
    digits = []
    for _ in range(4):
        quotient = jnp.floor(rest * (1.0 / Q))
        remainder = rest - quotient * Q
        over, under = remainder >= Q, remainder < 0.0
        quotient = jnp.where(over, quotient + 1.0, jnp.where(under, quotient - 1.0, quotient))
        remainder = jnp.where(over, remainder - Q, jnp.where(under, remainder + Q, remainder))
        digits.append(remainder)
        rest = quotient
    digits = jnp.concatenate(digits + [rest], axis=0).astype(BF16)

    def digit_residue(shape, dim):
        at = iota(shape, dim)
        line = at % 8
        return jnp.where(line < 6, 5 * line + at // 8, -1)

    lane_b = iota((40, 640), 1)
    block_b = jnp.where(lane_b < 320, core, 1 - core)
    local_b = jnp.where(lane_b < 320, lane_b, lane_b - 320)
    spread_b = digit_residue((40, 640), 0) == block_b * 15 + residue_of(local_b)
    own_digits = jnp.where(core == 0, digits[:, 0:256].astype(F32), digits[:, 256:512].astype(F32))
    value_b = dot(own_digits.astype(BF16), as_bf16(spread_b), ((0,), (0,)))
    local = jnp.where(lane_r < 320, lane_r, lane_r - 320)
    hot_b = (value_b == (local - residue_of(local) * Q).astype(F32)) & (local < 315)
    hot_b = as_bf16(hot_b)
    for g in row_groups:
        at = lanes(g)
        sums = dot(hot_b, j_high[:, at]) + dot(hot_b, j_low[:, at])
        xr[g][...] = sums.reshape(4, 2, 4, 8, -1)
        rows.step1(g)

    lane_c = iota((1, 384), 1)
    spread_c = digit_residue((40, 384), 0) == core * 15 + residue_of(iota((40, 384), 1))
    value_c = dot(digits, as_bf16(spread_c), ((0,), (0,)))
    hot_c = (value_c == (lane_c - residue_of(lane_c) * Q).astype(F32)) & (lane_c < 315)
    oc32[...] = hot_c.astype(F32).reshape(64, 8, 384)
    line_c = iota((320, 1), 0)
    spread_t = digit_residue((320, 40), 1) == core * 15 + residue_of(iota((320, 40), 0))
    value_t = dot(as_bf16(spread_t), digits)
    hot_t = (value_t == (line_c - residue_of(line_c) * Q).astype(F32)) & (line_c < 315)
    hot_t = as_bf16(hot_t)
    oct[0] = hot_t[:, 0:256]
    oct[1] = hot_t[:, 256:512]

    cols.step2(0)
    for g in row_groups:
        rows.step2(g)
    cols.step3(0)
    for g in row_groups:
        rows.step3(g)
    cols.step4(0)

    for g in row_groups:
        rows.step4(g)

    def line_weights(first):
        lane = iota((8, 512), 1) - iota((8, 512), 0)
        found = [jnp.where(lane == first + 32 * h + 8 * i, w_ref[...], 0.0) for h, i in first_blocks]
        return jnp.sum(jnp.concatenate(found, axis=0), axis=1, keepdims=True)

    def residual(energy, hot, residue, weight):
        member = as_bf16(iota((128, energy.shape[1]), 0) == residue)
        powers = jnp.exp(energy)
        lines = energy.shape[0]
        parts = dot(jnp.concatenate(three_parts(powers), axis=0), member, nt)
        sums = parts[0:lines] + parts[lines : 2 * lines] + parts[2 * lines :]
        inverse = jnp.where(sums > 0.0, 1.0 / sums, 0.0)
        parts = dot(jnp.concatenate(three_parts(inverse), axis=0), member)
        inverse = parts[0:lines] + parts[lines : 2 * lines] + parts[2 * lines :]
        return weight * (powers * inverse - hot)

    column, second, valid = packed_column(lane_r)
    residue_c = jnp.where(valid, residue_of(column) + jnp.where(second, 32, 0), -1)
    first = x * 64
    first_blocks = cols.blocks()

    def column_lines(start):
        return jnp.concatenate([oc32[start // 8 + 4 * h + i] for h, i in cols.blocks()], axis=0)

    hot1, hot2 = column_lines(first), column_lines(first + 256)
    hot = jnp.concatenate(
        [hot1[:, 0:256], hot2[:, 0:256], hot1[:, 256:384] + pltpu.roll(hot2[:, 256:384], 64, 1)],
        axis=1,
    )
    fields_c = jnp.where(core == 0, states[6:7, :], states[7:8, :])
    f_main, f_tail = fields_c[:, 0:256], jnp.broadcast_to(fields_c[:, 256:384], (8, 128))
    f_tail = (f_tail + pltpu.roll(f_tail, 64, 1))[0:1]
    fields_c = jnp.concatenate([f_main, f_main, f_tail], axis=1)
    weight = jnp.where(second, line_weights(first + 256), line_weights(first))
    cols.gather1(0, residual(cols.result(0) + fields_c, hot, residue_c, weight))

    block = core * 32 + y * 8
    first_blocks = rows.blocks()
    weight = line_weights(core * 256 + y * 64)
    fields_r = spread_lanes(fpad[...])[0:1]
    for g in row_groups:
        low, high = ROW_GROUPS[g]
        at = lanes(g)
        hot = jnp.concatenate([or32[block + 4 * h + i, :, at] for h, i in rows.blocks()], axis=0)
        energy = rows.result(g) + fields_r[:, low:high]
        rows.gather1(g, residual(energy, hot, res_r[:, low:high], weight))
        if g == 0:
            cols.gather2(0)
    cols.gather3(0)
    for g in row_groups:
        rows.gather2(g)

    cols.gathered(0)
    whole = wc[...].reshape(256, 640)
    tail = whole[:, 512:640]
    tail_lane = iota((1, 128), 1)
    tail1 = jnp.where(tail_lane < 64, tail, 0.0)
    tail2 = pltpu.roll(jnp.where(tail_lane < 64, 0.0, tail), 64, 1)
    first_c = jnp.concatenate([whole[:, 0:256], tail1], axis=1)
    second_c = jnp.concatenate([whole[:, 256:512], tail2], axis=1)

    def products(n, lines):
        hot = or32[32 * n : 32 * n + 32].reshape(256, 640).astype(BF16)
        return sum(dot(piece, hot, ((0,), (0,))) for piece in two_parts(lines))

    acc[...] = products(0, first_c)
    last = {g: [] for g in row_groups}

    def forward(i, h, g):
        piece = wr[g].at[core, i, h]
        last[g].append(exchange(piece, piece, partner))

    for g in row_groups:
        rows.gather3(g)
        for h in range(2):
            forward(y, h, g)
            forward(order(y, h)[1], h, g)
    acc[...] += products(1, second_c)
    for g in row_groups:
        rows.gathered(g)
        for h in range(2):
            forward(order(y, h)[0], h, g)
            forward(far(y), h, g)

    for n, ref in enumerate((f_ref, fm_ref, fs_ref)):
        field_ref[n : n + 1, 0:630] = ref[...].reshape(1, 630)

    def row_products(which, g):
        lines = wr[g][which].reshape(256, -1)
        hot = oct[which]
        acc[0:320, lanes(g)] += sum(dot(hot, piece) for piece in two_parts(lines))
        return jnp.sum(lines, axis=0, keepdims=True)

    def finish(t):
        high = min(128 * t + 128, 630)
        tile = natural_tile(lambda i: acc[0:320, 128 * i : 128 * i + 128], t)
        g_ref[:, 128 * t : high] = tile[0:315, 0 : high - 128 * t]

    line_sums = [row_products(core, g) for g in row_groups]
    done = 0
    for g in row_groups:
        for copy in last[g]:
            copy.wait_recv()
        fg_ref[0:1, lanes(g)] = line_sums[g] + row_products(1 - core, g)
        ready = ROW_GROUPS[g][1] // 128
        for t in range(done, ready - (ready < 5)):
            finish(t)
        done = ready - 1

    def grad_tile(i):
        return fg_ref[:, 128 * i : 128 * i + 128]

    grad = jnp.concatenate([natural_tile(grad_tile, t) for t in range(5)], axis=1)
    field_ref[3:4, :] = grad[0:1]

    for load in loads[6:]:
        load.wait()
    for copy in copies[-SENDS:]:
        copy.wait_send()

    @pl.when(row == owner)
    def _():
        for copy in state_copies:
            copy.wait_send()


def adam_update(values, first_moment, second_moment, gradient):
    first_new = 0.9 * first_moment + 0.1 * gradient
    second_new = 0.999 * second_moment + 0.001 * gradient * gradient
    root = jnp.sqrt(second_new * (1.0 / (1.0 - 0.999**10)))
    change = first_new * (0.05 / (1.0 - 0.9**10)) / (root + 1e-08)
    return (values - change, first_new, second_new)


def on_device(
    alignment, seq_weight, couplings, pair_mean, pair_square, fields, field_mean, field_square
):
    vmem = pl.BlockSpec(memory_space=pltpu.VMEM)

    def by_group(*dims):
        return [pltpu.VMEM((*dims, high - low), F32) for low, high in ROW_GROUPS]

    sums, field_lines, held_mean, held_square = pl.pallas_call(
        kernel,
        out_shape=(
            jax.ShapeDtypeStruct(couplings.shape[::-1], F32),
            jax.ShapeDtypeStruct((4, 640), F32),
            *[jax.ShapeDtypeStruct(couplings.shape[::-1], F32)] * 2,
        ),
        in_specs=[pl.BlockSpec(memory_space=pltpu.HBM)] * 8,
        out_specs=(vmem,) * 4,
        scratch_shapes=[
            pltpu.VMEM((8, 512), F32),
            pltpu.VMEM((64, 8, 384), F32),
            pltpu.VMEM((64, 8, 640), F32),
            pltpu.VMEM((2, 320, 256), BF16),
            pltpu.VMEM((320, 640), F32),
            pltpu.VMEM((640, 640), BF16),
            pltpu.VMEM((640, 640), BF16),
            pltpu.VMEM(couplings.shape[::-1], F32),
        ]
        + [by_group(4, 2, 4, 8), pltpu.VMEM((4, 2, 4, 8, 640), F32)]
        + [by_group(2, 2, 4, 8), by_group(2, 4, 8), by_group(2, 2, 8), by_group(2, 2, 8)]
        + [
            pltpu.VMEM((2, 2, 4, 8, 640), F32),
            pltpu.VMEM((2, 4, 8, 640), F32),
            pltpu.VMEM((2, 2, 8, 640), F32),
            pltpu.VMEM((2, 2, 8, 640), F32),
            by_group(2, 4, 2, 4, 8),
            pltpu.VMEM((4, 2, 4, 8, 640), F32),
            pltpu.VMEM((384, 640), F32),
            pltpu.VMEM((8, 640), F32),
            pltpu.VMEM((8, 640), F32),
            pltpu.VMEM(alignment.shape[::-1], jnp.int32),
            pltpu.VMEM((1, 512), F32),
            pltpu.VMEM(couplings.shape[::-1], F32),
            *[pltpu.VMEM(fields.shape, F32)] * 3,
            pltpu.SemaphoreType.DMA((8,)),
            pltpu.SemaphoreType.DMA((16,)),
            pltpu.SemaphoreType.DMA((SENDS,)),
            pltpu.SemaphoreType.DMA((20 + 26 * len(ROW_GROUPS),)),
        ],
        compiler_params=pltpu.CompilerParams(collective_id=0, has_side_effects=True, vmem_limit_bytes=VMEM_LIMIT),
    )(*(
        pltpu.with_memory_space_constraint(x, pltpu.HBM)
        for x in (
            alignment.T, seq_weight.reshape(1, -1), couplings.T,
            fields, field_mean, field_square, pair_mean.T, pair_square.T,
        )
    ))
    pair_mean, pair_square = held_mean.T, held_square.T
    sums = sums.T
    row_residues = alignment.shape[1]
    column_residues = couplings.shape[1] // Q
    row_ids = (
        lax.axis_index("row") * row_residues
        + lax.broadcasted_iota(jnp.int32, (couplings.shape[0], 1), 0) // Q
    )
    column_ids = (
        lax.axis_index("col") * column_residues
        + lax.broadcasted_iota(jnp.int32, (1, couplings.shape[1]), 1) // Q
    )
    pair_grad = jnp.where(row_ids != column_ids, sums, 0.0) + 0.2 * (L - 1) * couplings
    new_pairs, new_pair_mean, new_pair_square = adam_update(
        couplings, pair_mean, pair_square, pair_grad
    )
    new_fields, new_field_mean, new_field_square = adam_update(
        *(field_lines[n, : fields.shape[0]] for n in range(4))
    )
    return (new_pairs, new_pair_mean, new_pair_square, new_fields, new_field_mean, new_field_square)


def solution(mesh):
    block = P("row", "col")
    in_specs = (P(None, "row"), P(), block, block, block, P("row"), P("row"), P("row"))
    out_specs = (block, block, block, P("row"), P("row"), P("row"))
    return jax.shard_map(
        on_device, mesh=mesh, in_specs=in_specs, out_specs=out_specs, check_vma=False
    )
```

```python
import jax
import jax.numpy as jnp
from jax import lax
from jax.experimental import pallas as pl
from jax.experimental.pallas import tpu as pltpu
from jax.sharding import PartitionSpec as P

L = 480
Q = 21
MESH = pl.DeviceIdType.MESH
F32 = jnp.float32
BF16 = jnp.bfloat16
VMEM_LIMIT = 24 * 2**20
SENDS = 40
ROW_GROUPS = ((0, 384), (384, 640))


def two_parts(x):
    high = x.astype(BF16)
    return high, (x - high.astype(F32)).astype(BF16)


def three_parts(x):
    high = x.astype(BF16)
    rest = x - high.astype(F32)
    mid = rest.astype(BF16)
    return high, mid, (rest - mid.astype(F32)).astype(BF16)


def dot(a, b, dims=((1,), (0,))):
    return lax.dot_general(a, b, (dims, ((), ())), preferred_element_type=F32)


def residue_of(lane):
    return ((lane.astype(F32) + 0.5) * (1.0 / Q)).astype(jnp.int32)


def flip(i):
    return i + 1 - 2 * (i % 2)


def mirror(i):
    return 3 - i


def packed_column(lane):
    main = jnp.where(lane < 256, lane, lane - 256)
    tail = jnp.where(lane < 576, lane - 512, lane - 576)
    column = jnp.where(lane < 512, main, tail + 256)
    second = ((lane >= 256) & (lane < 512)) | (lane >= 576)
    return column, second, (lane < 512) | (tail < 59)


def iota(shape, dim):
    return lax.broadcasted_iota(jnp.int32, shape, dim)


def as_bf16(mask):
    return mask.astype(F32).astype(BF16)


def order(i, half):
    first, second = flip(i), mirror(i)
    return (first, second) if half == 0 else (second, first)


def far(i):
    return (i + 2) % 4


def spread_lanes(x):
    at = iota((1, 128), 1)
    tiles = [x[:, 0:128]]
    for t in range(1, 5):
        last, this = x[:, 128 * t - 128 : 128 * t], x[:, 128 * t : 128 * t + 128]
        tiles.append(jnp.where(at < 2 * t, pltpu.roll(last, 2 * t, 1), pltpu.roll(this, 2 * t, 1)))
    return jnp.concatenate(tiles, axis=1)


def natural_tile(tile, t):
    at = iota((1, 128), 1)
    this = tile(t) if t == 0 else pltpu.roll(tile(t), 128 - 2 * t, 1)
    if t == 4:
        return this
    return jnp.where(at < 126 - 2 * t, this, pltpu.roll(tile(t + 1), 126 - 2 * t, 1))


class Reduce:
    def __init__(self, exchange, a, b, at, total, ins, full):
        self.exchange, self.a, self.b, self.at = exchange, a, b, at
        self.total, self.ins, self.full = total, ins, full
        self.s1, self.s2, self.s3, self.s4 = {}, {}, {}, {}
        self.g1, self.g2, self.g3 = {}, {}, {}

    def step1(self, g):
        for h in range(2):
            p, _ = order(self.a, h)
            to = self.at(p, self.b)
            later = self.total[g].at[far(self.a), h]
            theirs = self.total[g].at[p, h]
            one = self.exchange(later, self.ins[0][g].at[h, 1], to)
            two = self.exchange(theirs, self.ins[0][g].at[h, 0], to)
            self.s1[g, h] = (two, one)

    def step2(self, g):
        for h in range(2):
            p, q = order(self.a, h)
            self.s1[g, h][1].wait_recv()
            self.total[g][q, h] += self.ins[0][g][h, 1]
            self.s2[g, h] = self.exchange(
                self.total[g].at[q, h], self.ins[1][g].at[h], self.at(q, self.b)
            )
        for h in range(2):
            self.s1[g, h][0].wait_recv()
            self.total[g][self.a, h] += self.ins[0][g][h, 0]

    def pair(self, h, i):
        at = (i + 1) % 4 if h == 0 else i
        return at - at % 2

    def step3(self, g):
        for h in range(2):
            p, _ = order(self.b, h)
            self.s2[g, h].wait_recv()
            self.total[g][self.a, h] += self.ins[1][g][h]
            theirs = self.total[g].at[self.a, h, pl.ds(self.pair(h, p), 2)]
            self.s3[g, h] = self.exchange(theirs, self.ins[2][g].at[h], self.at(self.a, p))

    def step4(self, g):
        for h in range(2):
            _, q = order(self.b, h)
            mine = pl.ds(self.pair(h, self.b), 2)
            self.s3[g, h].wait_recv()
            self.total[g][self.a, h, mine] += self.ins[2][g][h]
            self.s4[g, h] = self.exchange(
                self.total[g].at[self.a, h, mine], self.ins[3][g].at[h], self.at(self.a, q)
            )

    def blocks(self):
        return [(h, self.pair(h, self.b) + n) for h in range(2) for n in range(2)]

    def result(self, g):
        for h in range(2):
            self.s4[g, h].wait_recv()
        parts = [
            self.total[g][self.a, h, i] + self.ins[3][g][h, n % 2]
            for n, (h, i) in enumerate(self.blocks())
        ]
        return jnp.concatenate(parts, axis=0)

    def gather1(self, g, value):
        for n, (h, i) in enumerate(self.blocks()):
            self.full[g][self.a, h, i] = value[8 * n : 8 * n + 8]
        for h in range(2):
            p, _ = order(self.b, h)
            mine = self.full[g].at[self.a, h, pl.ds(self.pair(h, self.b), 2)]
            self.g1[g, h] = self.exchange(mine, mine, self.at(self.a, p))

    def gather2(self, g):
        for h in range(2):
            p, q = order(self.a, h)
            self.g1[g, h].wait_recv()
            own = self.full[g].at[self.a, h]
            self.g2[g, h] = self.exchange(own, own, self.at(q, self.b))
            self.g3[g, h] = [self.exchange(own, own, self.at(p, self.b))]

    def gather3(self, g):
        for h in range(2):
            p, q = order(self.a, h)
            second = self.full[g].at[q, h]
            self.g2[g, h].wait_recv()
            self.g3[g, h].append(self.exchange(second, second, self.at(p, self.b)))

    def gathered(self, g):
        for h in range(2):
            for copy in self.g3[g, h]:
                copy.wait_recv()


def kernel(
    al_in, w_in, j_ref, f_in, fm_in, fs_in, pm_in, ps_in, g_ref, field_ref, pm_ref, ps_ref,
    states, oc32, or32, oct, j_pad, j_high, j_low, j_in, xr, xc,
    r_in1, r_in2, r_in3, r_in4, c_in1, c_in2, c_in3, c_in4, wr, wc, acc,
    fpad, fg_ref, al_ref, w_ref, j_own, f_ref, fm_ref, fs_ref, local, state_send, send, recv,
):
    row, col = lax.axis_index("row"), lax.axis_index("col")
    z_lo, x = row // 4, row % 4
    y, z_hi, core = col // 8, (col // 2) % 4, col % 2
    owner = col // 2

    def at_row(a, b):
        return (row, a * 8 + b * 2 + core)

    def at_col(a, b):
        return (b * 4 + a, col)

    partner = (row, y * 8 + z_hi * 2 + 1 - core)

    loads = [
        pltpu.make_async_copy(src, dst, local.at[n])
        for n, (src, dst) in enumerate(
            ((al_in, al_ref), (f_in, f_ref), (j_ref, j_own), (w_in, w_ref), (fm_in, fm_ref), (fs_in, fs_ref), (pm_in, pm_ref), (ps_in, ps_ref))
        )
    ]
    for load in loads:
        load.start()

    barrier = pltpu.get_barrier_semaphore()
    greeted = [at_row(flip(y), z_hi), at_row(mirror(y), z_hi), at_row(y, flip(z_hi))]
    greeted += [at_row(y, mirror(z_hi)), partner]
    greeted += [((row + d) % 16, col) for d in range(1, 16)]
    for device in greeted:
        pl.semaphore_signal(barrier, inc=1, device_id=device, device_id_type=MESH)

    loads[0].wait()
    loads[1].wait()

    fpad[...] = jnp.zeros_like(fpad)
    fg_ref[...] = jnp.zeros_like(fg_ref)
    fpad[0:1, 0:630] = f_ref[...].reshape(1, 630)
    fields = fpad[...]
    field_lane = iota((8, 640), 1)
    fields0 = jnp.where(field_lane < 315, fields, 0.0)[0:1, 0:512]
    fields1 = jnp.where(field_lane < 315, pltpu.roll(fields, 325, 1), 0.0)[0:1, 0:512]
    alignment = al_ref[...].astype(F32).astype(BF16)
    word_row, word_residue = iota((8, 30), 0), iota((8, 30), 1)
    digit = word_residue - 5 * word_row
    scale = jnp.zeros((8, 30), F32)
    for d in range(5):
        scale = jnp.where(digit == d, float(Q**d), scale)
    words = sum(dot(part, alignment) for part in three_parts(scale))
    word_line = iota((8, 512), 0)
    words = jnp.where(word_line == 6, fields0, jnp.where(word_line == 7, fields1, words))

    loads[2].wait()
    for load in loads[3:6]:
        load.wait()
    j_pad[...] = jnp.zeros_like(j_pad)
    j_pad[0:315, 0:630] = j_own[...]
    high, low = two_parts(spread_lanes(j_pad[...]))
    j_high[0:320, :] = high
    j_low[0:320, :] = low

    lane_r = iota((1, 640), 1)

    def tile_residue(lane):
        tile = lane // 128
        return tile * 6 + residue_of(lane - tile * 128)

    inside = lane_r % 128 < 126
    res_r = jnp.where(inside, tile_residue(lane_r), -1)
    state_r = (lane_r % 128) - residue_of(lane_r % 128) * Q
    spread_r = iota((30, 640), 0) == tile_residue(iota((30, 640), 1))
    value_r = dot(alignment, as_bf16(spread_r), ((0,), (0,)))
    hot_r = (value_r == state_r.astype(F32)) & inside
    hot_r = hot_r.astype(F32)
    or32[...] = hot_r.reshape(64, 8, 640)
    hot_r = hot_r.astype(BF16)

    nt = ((1,), (1,))
    top, bottom = hot_r[0:256], hot_r[256:512]
    none = jnp.zeros((64, 640), BF16)
    tails = [j[256:320] for j in (j_high, j_low)]
    tails1 = [jnp.concatenate([tail, none], axis=0) for tail in tails]
    tails2 = [jnp.concatenate([none, tail], axis=0) for tail in tails]
    mains = [j[0:256] for j in (j_high, j_low)]
    xc[:, :, :, :, 0:256] = sum(dot(top, j, nt) for j in mains).reshape(4, 2, 4, 8, 256)
    xc[:, :, :, :, 256:512] = sum(dot(bottom, j, nt) for j in mains).reshape(4, 2, 4, 8, 256)
    xc[:, :, :, :, 512:640] = (
        sum(dot(top, j, nt) for j in tails1) + sum(dot(bottom, j, nt) for j in tails2)
    ).reshape(4, 2, 4, 8, 128)

    pl.semaphore_wait(barrier, len(greeted))

    state_copies = [
        pltpu.make_async_remote_copy(
            states, states, state_send.at[d], recv.at[0],
            device_id=((row + d) % 16, col), device_id_type=MESH,
        )
        for d in range(1, 16)
    ]

    @pl.when(row == owner)
    def _():
        states[...] = words
        for copy in state_copies:
            copy.start()

    copies = []

    def exchange(src, dst, device):
        at = len(copies)
        if at >= SENDS:
            copies[at - SENDS].wait_send()
        copy = pltpu.make_async_remote_copy(
            src, dst, send.at[at % SENDS], recv.at[at + 1], device_id=device, device_id_type=MESH
        )
        copy.start()
        copies.append(copy)
        return copy

    across = exchange(j_ref, j_in, partner)
    cols = Reduce(
        exchange, x, z_lo, at_col, [xc], ([c_in1], [c_in2], [c_in3], [c_in4]), [wc]
    )
    rows = Reduce(
        exchange, y, z_hi, at_row, xr, (r_in1, r_in2, r_in3, r_in4), [w.at[core] for w in wr]
    )
    row_groups = range(len(ROW_GROUPS))

    def lanes(g):
        return slice(*ROW_GROUPS[g])

    cols.step1(0)

    across.wait_recv()
    j_pad[0:315, 0:630] = j_in[...]
    high, low = two_parts(spread_lanes(j_pad[...]))
    j_high[320:640, :] = high
    j_low[320:640, :] = low

    @pl.when(row != owner)
    def _():
        state_copies[0].wait_recv()

    rest = jnp.where(word_line < 6, states[...], 0.0)
    digits = []
    for _ in range(4):
        quotient = jnp.floor(rest * (1.0 / Q))
        remainder = rest - quotient * Q
        over, under = remainder >= Q, remainder < 0.0
        quotient = jnp.where(over, quotient + 1.0, jnp.where(under, quotient - 1.0, quotient))
        remainder = jnp.where(over, remainder - Q, jnp.where(under, remainder + Q, remainder))
        digits.append(remainder)
        rest = quotient
    digits = jnp.concatenate(digits + [rest], axis=0).astype(BF16)

    def digit_residue(shape, dim):
        at = iota(shape, dim)
        line = at % 8
        return jnp.where(line < 6, 5 * line + at // 8, -1)

    lane_b = iota((40, 640), 1)
    block_b = jnp.where(lane_b < 320, core, 1 - core)
    local_b = jnp.where(lane_b < 320, lane_b, lane_b - 320)
    spread_b = digit_residue((40, 640), 0) == block_b * 15 + residue_of(local_b)
    own_digits = jnp.where(core == 0, digits[:, 0:256].astype(F32), digits[:, 256:512].astype(F32))
    value_b = dot(own_digits.astype(BF16), as_bf16(spread_b), ((0,), (0,)))
    local = jnp.where(lane_r < 320, lane_r, lane_r - 320)
    hot_b = (value_b == (local - residue_of(local) * Q).astype(F32)) & (local < 315)
    hot_b = as_bf16(hot_b)
    for g in row_groups:
        at = lanes(g)
        sums = dot(hot_b, j_high[:, at]) + dot(hot_b, j_low[:, at])
        xr[g][...] = sums.reshape(4, 2, 4, 8, -1)
        rows.step1(g)

    cols.step2(0)

    lane_c = iota((1, 384), 1)
    spread_c = digit_residue((40, 384), 0) == core * 15 + residue_of(iota((40, 384), 1))
    value_c = dot(digits, as_bf16(spread_c), ((0,), (0,)))
    hot_c = (value_c == (lane_c - residue_of(lane_c) * Q).astype(F32)) & (lane_c < 315)
    oc32[...] = hot_c.astype(F32).reshape(64, 8, 384)
    line_c = iota((320, 1), 0)
    spread_t = digit_residue((320, 40), 1) == core * 15 + residue_of(iota((320, 40), 0))
    value_t = dot(as_bf16(spread_t), digits)
    hot_t = (value_t == (line_c - residue_of(line_c) * Q).astype(F32)) & (line_c < 315)
    hot_t = as_bf16(hot_t)
    oct[0] = hot_t[:, 0:256]
    oct[1] = hot_t[:, 256:512]

    cols.step3(0)
    for g in row_groups:
        rows.step2(g)
    cols.step4(0)
    for g in row_groups:
        rows.step3(g)

    def line_weights(first):
        lane = iota((8, 512), 1) - iota((8, 512), 0)
        found = [jnp.where(lane == first + 32 * h + 8 * i, w_ref[...], 0.0) for h, i in first_blocks]
        return jnp.sum(jnp.concatenate(found, axis=0), axis=1, keepdims=True)

    def residual(energy, hot, residue, weight):
        member = as_bf16(iota((128, energy.shape[1]), 0) == residue)
        powers = jnp.exp(energy)
        lines = energy.shape[0]
        parts = dot(jnp.concatenate(three_parts(powers), axis=0), member, nt)
        sums = parts[0:lines] + parts[lines : 2 * lines] + parts[2 * lines :]
        inverse = jnp.where(sums > 0.0, 1.0 / sums, 0.0)
        parts = dot(jnp.concatenate(three_parts(inverse), axis=0), member)
        inverse = parts[0:lines] + parts[lines : 2 * lines] + parts[2 * lines :]
        return weight * (powers * inverse - hot)

    column, second, valid = packed_column(lane_r)
    residue_c = jnp.where(valid, residue_of(column) + jnp.where(second, 32, 0), -1)
    first = x * 64
    first_blocks = cols.blocks()

    def column_lines(start):
        return jnp.concatenate([oc32[start // 8 + 4 * h + i] for h, i in cols.blocks()], axis=0)

    hot1, hot2 = column_lines(first), column_lines(first + 256)
    hot = jnp.concatenate(
        [hot1[:, 0:256], hot2[:, 0:256], hot1[:, 256:384] + pltpu.roll(hot2[:, 256:384], 64, 1)],
        axis=1,
    )
    fields_c = jnp.where(core == 0, states[6:7, :], states[7:8, :])
    f_main, f_tail = fields_c[:, 0:256], jnp.broadcast_to(fields_c[:, 256:384], (8, 128))
    f_tail = (f_tail + pltpu.roll(f_tail, 64, 1))[0:1]
    fields_c = jnp.concatenate([f_main, f_main, f_tail], axis=1)
    weight = jnp.where(second, line_weights(first + 256), line_weights(first))
    cols.gather1(0, residual(cols.result(0) + fields_c, hot, residue_c, weight))
    for g in row_groups:
        rows.step4(g)
    cols.gather2(0)

    block = core * 32 + y * 8
    first_blocks = rows.blocks()
    weight = line_weights(core * 256 + y * 64)
    fields_r = spread_lanes(fpad[...])[0:1]
    for g in row_groups:
        low, high = ROW_GROUPS[g]
        at = lanes(g)
        hot = jnp.concatenate([or32[block + 4 * h + i, :, at] for h, i in rows.blocks()], axis=0)
        energy = rows.result(g) + fields_r[:, low:high]
        rows.gather1(g, residual(energy, hot, res_r[:, low:high], weight))
    cols.gather3(0)
    for g in row_groups:
        rows.gather2(g)

    cols.gathered(0)
    whole = wc[...].reshape(256, 640)
    tail = whole[:, 512:640]
    tail_lane = iota((1, 128), 1)
    tail1 = jnp.where(tail_lane < 64, tail, 0.0)
    tail2 = pltpu.roll(jnp.where(tail_lane < 64, 0.0, tail), 64, 1)
    first_c = jnp.concatenate([whole[:, 0:256], tail1], axis=1)
    second_c = jnp.concatenate([whole[:, 256:512], tail2], axis=1)

    def products(n, lines):
        hot = or32[32 * n : 32 * n + 32].reshape(256, 640).astype(BF16)
        return sum(dot(piece, hot, ((0,), (0,))) for piece in two_parts(lines))

    acc[...] = products(0, first_c)
    last = {g: [] for g in row_groups}

    def forward(i, h, g):
        piece = wr[g].at[core, i, h]
        last[g].append(exchange(piece, piece, partner))

    for g in row_groups:
        rows.gather3(g)
        for h in range(2):
            forward(y, h, g)
            forward(order(y, h)[1], h, g)
    acc[...] += products(1, second_c)
    for g in row_groups:
        rows.gathered(g)
        for h in range(2):
            forward(order(y, h)[0], h, g)
            forward(far(y), h, g)

    for n, ref in enumerate((f_ref, fm_ref, fs_ref)):
        field_ref[n : n + 1, 0:630] = ref[...].reshape(1, 630)

    def row_products(which, g):
        lines = wr[g][which].reshape(256, -1)
        hot = oct[which]
        acc[0:320, lanes(g)] += sum(dot(hot, piece) for piece in two_parts(lines))
        return jnp.sum(lines, axis=0, keepdims=True)

    def finish(t):
        high = min(128 * t + 128, 630)
        tile = natural_tile(lambda i: acc[0:320, 128 * i : 128 * i + 128], t)
        g_ref[:, 128 * t : high] = tile[0:315, 0 : high - 128 * t]

    line_sums = [row_products(core, g) for g in row_groups]
    done = 0
    for g in row_groups:
        for copy in last[g]:
            copy.wait_recv()
        fg_ref[0:1, lanes(g)] = line_sums[g] + row_products(1 - core, g)
        ready = ROW_GROUPS[g][1] // 128
        for t in range(done, ready - (ready < 5)):
            finish(t)
        done = ready - 1

    def grad_tile(i):
        return fg_ref[:, 128 * i : 128 * i + 128]

    grad = jnp.concatenate([natural_tile(grad_tile, t) for t in range(5)], axis=1)
    field_ref[3:4, :] = grad[0:1]

    for load in loads[6:]:
        load.wait()
    for copy in copies[-SENDS:]:
        copy.wait_send()

    @pl.when(row == owner)
    def _():
        for copy in state_copies:
            copy.wait_send()


def adam_update(values, first_moment, second_moment, gradient):
    first_new = 0.9 * first_moment + 0.1 * gradient
    second_new = 0.999 * second_moment + 0.001 * gradient * gradient
    root = jnp.sqrt(second_new * (1.0 / (1.0 - 0.999**10)))
    change = first_new * (0.05 / (1.0 - 0.9**10)) / (root + 1e-08)
    return (values - change, first_new, second_new)


def on_device(
    alignment, seq_weight, couplings, pair_mean, pair_square, fields, field_mean, field_square
):
    vmem = pl.BlockSpec(memory_space=pltpu.VMEM)

    def by_group(*dims):
        return [pltpu.VMEM((*dims, high - low), F32) for low, high in ROW_GROUPS]

    sums, field_lines, held_mean, held_square = pl.pallas_call(
        kernel,
        out_shape=(
            jax.ShapeDtypeStruct(couplings.shape[::-1], F32),
            jax.ShapeDtypeStruct((4, 640), F32),
            *[jax.ShapeDtypeStruct(couplings.shape[::-1], F32)] * 2,
        ),
        in_specs=[pl.BlockSpec(memory_space=pltpu.HBM)] * 8,
        out_specs=(vmem,) * 4,
        scratch_shapes=[
            pltpu.VMEM((8, 512), F32),
            pltpu.VMEM((64, 8, 384), F32),
            pltpu.VMEM((64, 8, 640), F32),
            pltpu.VMEM((2, 320, 256), BF16),
            pltpu.VMEM((320, 640), F32),
            pltpu.VMEM((640, 640), BF16),
            pltpu.VMEM((640, 640), BF16),
            pltpu.VMEM(couplings.shape[::-1], F32),
        ]
        + [by_group(4, 2, 4, 8), pltpu.VMEM((4, 2, 4, 8, 640), F32)]
        + [by_group(2, 2, 4, 8), by_group(2, 4, 8), by_group(2, 2, 8), by_group(2, 2, 8)]
        + [
            pltpu.VMEM((2, 2, 4, 8, 640), F32),
            pltpu.VMEM((2, 4, 8, 640), F32),
            pltpu.VMEM((2, 2, 8, 640), F32),
            pltpu.VMEM((2, 2, 8, 640), F32),
            by_group(2, 4, 2, 4, 8),
            pltpu.VMEM((4, 2, 4, 8, 640), F32),
            pltpu.VMEM((384, 640), F32),
            pltpu.VMEM((8, 640), F32),
            pltpu.VMEM((8, 640), F32),
            pltpu.VMEM(alignment.shape[::-1], jnp.int32),
            pltpu.VMEM((1, 512), F32),
            pltpu.VMEM(couplings.shape[::-1], F32),
            *[pltpu.VMEM(fields.shape, F32)] * 3,
            pltpu.SemaphoreType.DMA((8,)),
            pltpu.SemaphoreType.DMA((16,)),
            pltpu.SemaphoreType.DMA((SENDS,)),
            pltpu.SemaphoreType.DMA((20 + 26 * len(ROW_GROUPS),)),
        ],
        compiler_params=pltpu.CompilerParams(collective_id=0, has_side_effects=True, vmem_limit_bytes=VMEM_LIMIT),
    )(*(
        pltpu.with_memory_space_constraint(x, pltpu.HBM)
        for x in (
            alignment.T, seq_weight.reshape(1, -1), couplings.T,
            fields, field_mean, field_square, pair_mean.T, pair_square.T,
        )
    ))
    pair_mean, pair_square = held_mean.T, held_square.T
    sums = sums.T
    row_residues = alignment.shape[1]
    column_residues = couplings.shape[1] // Q
    row_ids = (
        lax.axis_index("row") * row_residues
        + lax.broadcasted_iota(jnp.int32, (couplings.shape[0], 1), 0) // Q
    )
    column_ids = (
        lax.axis_index("col") * column_residues
        + lax.broadcasted_iota(jnp.int32, (1, couplings.shape[1]), 1) // Q
    )
    pair_grad = jnp.where(row_ids != column_ids, sums, 0.0) + 0.2 * (L - 1) * couplings
    new_pairs, new_pair_mean, new_pair_square = adam_update(
        couplings, pair_mean, pair_square, pair_grad
    )
    new_fields, new_field_mean, new_field_square = adam_update(
        *(field_lines[n, : fields.shape[0]] for n in range(4))
    )
    return (new_pairs, new_pair_mean, new_pair_square, new_fields, new_field_mean, new_field_square)


def solution(mesh):
    block = P("row", "col")
    in_specs = (P(None, "row"), P(), block, block, block, P("row"), P("row"), P("row"))
    out_specs = (block, block, block, P("row"), P("row"), P("row"))
    return jax.shard_map(
        on_device, mesh=mesh, in_specs=in_specs, out_specs=out_specs, check_vma=False
    )
```

```python
import jax
import jax.numpy as jnp
from jax import lax
from jax.experimental import pallas as pl
from jax.experimental.pallas import tpu as pltpu
from jax.sharding import PartitionSpec as P

L = 480
Q = 21
MESH = pl.DeviceIdType.MESH
F32 = jnp.float32
BF16 = jnp.bfloat16
VMEM_LIMIT = 24 * 2**20
SENDS = 40
ROW_GROUPS = ((0, 384), (384, 640))


def two_parts(x):
    high = x.astype(BF16)
    return high, (x - high.astype(F32)).astype(BF16)


def three_parts(x):
    high = x.astype(BF16)
    rest = x - high.astype(F32)
    mid = rest.astype(BF16)
    return high, mid, (rest - mid.astype(F32)).astype(BF16)


def dot(a, b, dims=((1,), (0,))):
    return lax.dot_general(a, b, (dims, ((), ())), preferred_element_type=F32)


def residue_of(lane):
    return ((lane.astype(F32) + 0.5) * (1.0 / Q)).astype(jnp.int32)


def flip(i):
    return i + 1 - 2 * (i % 2)


def mirror(i):
    return 3 - i


def packed_column(lane):
    main = jnp.where(lane < 256, lane, lane - 256)
    tail = jnp.where(lane < 576, lane - 512, lane - 576)
    column = jnp.where(lane < 512, main, tail + 256)
    second = ((lane >= 256) & (lane < 512)) | (lane >= 576)
    return column, second, (lane < 512) | (tail < 59)


def iota(shape, dim):
    return lax.broadcasted_iota(jnp.int32, shape, dim)


def as_bf16(mask):
    return mask.astype(F32).astype(BF16)


def order(i, half):
    first, second = flip(i), mirror(i)
    return (first, second) if half == 0 else (second, first)


def far(i):
    return (i + 2) % 4


def spread_lanes(x):
    at = iota((1, 128), 1)
    tiles = [x[:, 0:128]]
    for t in range(1, 5):
        last, this = x[:, 128 * t - 128 : 128 * t], x[:, 128 * t : 128 * t + 128]
        tiles.append(jnp.where(at < 2 * t, pltpu.roll(last, 2 * t, 1), pltpu.roll(this, 2 * t, 1)))
    return jnp.concatenate(tiles, axis=1)


def natural_tile(tile, t):
    at = iota((1, 128), 1)
    this = tile(t) if t == 0 else pltpu.roll(tile(t), 128 - 2 * t, 1)
    if t == 4:
        return this
    return jnp.where(at < 126 - 2 * t, this, pltpu.roll(tile(t + 1), 126 - 2 * t, 1))


class Reduce:
    def __init__(self, exchange, a, b, at, total, ins, full):
        self.exchange, self.a, self.b, self.at = exchange, a, b, at
        self.total, self.ins, self.full = total, ins, full
        self.s1, self.s2, self.s3, self.s4 = {}, {}, {}, {}
        self.g1, self.g2, self.g3 = {}, {}, {}

    def step1(self, g):
        for h in range(2):
            p, _ = order(self.a, h)
            to = self.at(p, self.b)
            later = self.total[g].at[far(self.a), h]
            theirs = self.total[g].at[p, h]
            one = self.exchange(later, self.ins[0][g].at[h, 1], to)
            two = self.exchange(theirs, self.ins[0][g].at[h, 0], to)
            self.s1[g, h] = (two, one)

    def step2(self, g):
        for h in range(2):
            p, q = order(self.a, h)
            self.s1[g, h][1].wait_recv()
            self.total[g][q, h] += self.ins[0][g][h, 1]
            self.s2[g, h] = self.exchange(
                self.total[g].at[q, h], self.ins[1][g].at[h], self.at(q, self.b)
            )
        for h in range(2):
            self.s1[g, h][0].wait_recv()
            self.total[g][self.a, h] += self.ins[0][g][h, 0]

    def pair(self, h, i):
        at = (i + 1) % 4 if h == 0 else i
        return at - at % 2

    def step3(self, g):
        for h in range(2):
            p, _ = order(self.b, h)
            self.s2[g, h].wait_recv()
            self.total[g][self.a, h] += self.ins[1][g][h]
            theirs = self.total[g].at[self.a, h, pl.ds(self.pair(h, p), 2)]
            self.s3[g, h] = self.exchange(theirs, self.ins[2][g].at[h], self.at(self.a, p))

    def step4(self, g):
        for h in range(2):
            _, q = order(self.b, h)
            mine = pl.ds(self.pair(h, self.b), 2)
            self.s3[g, h].wait_recv()
            self.total[g][self.a, h, mine] += self.ins[2][g][h]
            self.s4[g, h] = self.exchange(
                self.total[g].at[self.a, h, mine], self.ins[3][g].at[h], self.at(self.a, q)
            )

    def blocks(self):
        return [(h, self.pair(h, self.b) + n) for h in range(2) for n in range(2)]

    def result(self, g):
        for h in range(2):
            self.s4[g, h].wait_recv()
        parts = [
            self.total[g][self.a, h, i] + self.ins[3][g][h, n % 2]
            for n, (h, i) in enumerate(self.blocks())
        ]
        return jnp.concatenate(parts, axis=0)

    def gather1(self, g, value):
        for n, (h, i) in enumerate(self.blocks()):
            self.full[g][self.a, h, i] = value[8 * n : 8 * n + 8]
        for h in range(2):
            p, _ = order(self.b, h)
            mine = self.full[g].at[self.a, h, pl.ds(self.pair(h, self.b), 2)]
            self.g1[g, h] = self.exchange(mine, mine, self.at(self.a, p))

    def gather2(self, g):
        for h in range(2):
            p, q = order(self.a, h)
            self.g1[g, h].wait_recv()
            own = self.full[g].at[self.a, h]
            self.g2[g, h] = self.exchange(own, own, self.at(q, self.b))
            self.g3[g, h] = [self.exchange(own, own, self.at(p, self.b))]

    def gather3(self, g):
        for h in range(2):
            p, q = order(self.a, h)
            second = self.full[g].at[q, h]
            self.g2[g, h].wait_recv()
            self.g3[g, h].append(self.exchange(second, second, self.at(p, self.b)))

    def gathered(self, g):
        for h in range(2):
            for copy in self.g3[g, h]:
                copy.wait_recv()


def kernel(
    al_in, w_in, j_ref, f_in, fm_in, fs_in, pm_in, ps_in, g_ref, field_ref, pm_ref, ps_ref,
    states, oc32, or32, oct, j_pad, j_high, j_low, j_in, xr, xc,
    r_in1, r_in2, r_in3, r_in4, c_in1, c_in2, c_in3, c_in4, wr, wc, acc,
    fpad, fg_ref, al_ref, w_ref, j_own, f_ref, fm_ref, fs_ref, local, state_send, send, recv,
):
    row, col = lax.axis_index("row"), lax.axis_index("col")
    z_lo, x = row // 4, row % 4
    y, z_hi, core = col // 8, (col // 2) % 4, col % 2
    owner = col // 2

    def at_row(a, b):
        return (row, a * 8 + b * 2 + core)

    def at_col(a, b):
        return (b * 4 + a, col)

    partner = (row, y * 8 + z_hi * 2 + 1 - core)

    loads = [
        pltpu.make_async_copy(src, dst, local.at[n])
        for n, (src, dst) in enumerate(
            ((al_in, al_ref), (f_in, f_ref), (j_ref, j_own), (w_in, w_ref), (fm_in, fm_ref), (fs_in, fs_ref), (pm_in, pm_ref), (ps_in, ps_ref))
        )
    ]
    for load in loads:
        load.start()

    barrier = pltpu.get_barrier_semaphore()
    greeted = [at_row(flip(y), z_hi), at_row(mirror(y), z_hi), at_row(y, flip(z_hi))]
    greeted += [at_row(y, mirror(z_hi)), partner]
    greeted += [((row + d) % 16, col) for d in range(1, 16)]
    for device in greeted:
        pl.semaphore_signal(barrier, inc=1, device_id=device, device_id_type=MESH)

    loads[0].wait()
    loads[1].wait()

    fpad[...] = jnp.zeros_like(fpad)
    fg_ref[...] = jnp.zeros_like(fg_ref)
    fpad[0:1, 0:630] = f_ref[...].reshape(1, 630)
    fields = fpad[...]
    field_lane = iota((8, 640), 1)
    fields0 = jnp.where(field_lane < 315, fields, 0.0)[0:1, 0:512]
    fields1 = jnp.where(field_lane < 315, pltpu.roll(fields, 325, 1), 0.0)[0:1, 0:512]
    alignment = al_ref[...].astype(F32).astype(BF16)
    word_row, word_residue = iota((8, 30), 0), iota((8, 30), 1)
    digit = word_residue - 5 * word_row
    scale = jnp.zeros((8, 30), F32)
    for d in range(5):
        scale = jnp.where(digit == d, float(Q**d), scale)
    words = sum(dot(part, alignment) for part in three_parts(scale))
    word_line = iota((8, 512), 0)
    words = jnp.where(word_line == 6, fields0, jnp.where(word_line == 7, fields1, words))

    loads[2].wait()
    for load in loads[3:6]:
        load.wait()
    j_pad[...] = jnp.zeros_like(j_pad)
    j_pad[0:315, 0:630] = j_own[...]
    high, low = two_parts(spread_lanes(j_pad[...]))
    j_high[0:320, :] = high
    j_low[0:320, :] = low

    lane_r = iota((1, 640), 1)

    def tile_residue(lane):
        tile = lane // 128
        return tile * 6 + residue_of(lane - tile * 128)

    inside = lane_r % 128 < 126
    res_r = jnp.where(inside, tile_residue(lane_r), -1)
    state_r = (lane_r % 128) - residue_of(lane_r % 128) * Q
    spread_r = iota((30, 640), 0) == tile_residue(iota((30, 640), 1))
    value_r = dot(alignment, as_bf16(spread_r), ((0,), (0,)))
    hot_r = (value_r == state_r.astype(F32)) & inside
    hot_r = hot_r.astype(F32)
    or32[...] = hot_r.reshape(64, 8, 640)
    hot_r = hot_r.astype(BF16)

    pl.semaphore_wait(barrier, len(greeted))

    state_copies = [
        pltpu.make_async_remote_copy(
            states, states, state_send.at[d], recv.at[0],
            device_id=((row + d) % 16, col), device_id_type=MESH,
        )
        for d in range(1, 16)
    ]

    @pl.when(row == owner)
    def _():
        states[...] = words
        for copy in state_copies:
            copy.start()

    copies = []

    def exchange(src, dst, device):
        at = len(copies)
        if at >= SENDS:
            copies[at - SENDS].wait_send()
        copy = pltpu.make_async_remote_copy(
            src, dst, send.at[at % SENDS], recv.at[at + 1], device_id=device, device_id_type=MESH
        )
        copy.start()
        copies.append(copy)
        return copy

    across = exchange(j_ref, j_in, partner)
    nt = ((1,), (1,))
    top, bottom = hot_r[0:256], hot_r[256:512]
    none = jnp.zeros((64, 640), BF16)
    tails = [j[256:320] for j in (j_high, j_low)]
    tails1 = [jnp.concatenate([tail, none], axis=0) for tail in tails]
    tails2 = [jnp.concatenate([none, tail], axis=0) for tail in tails]
    mains = [j[0:256] for j in (j_high, j_low)]
    xc[:, :, :, :, 0:256] = sum(dot(top, j, nt) for j in mains).reshape(4, 2, 4, 8, 256)
    xc[:, :, :, :, 256:512] = sum(dot(bottom, j, nt) for j in mains).reshape(4, 2, 4, 8, 256)
    xc[:, :, :, :, 512:640] = (
        sum(dot(top, j, nt) for j in tails1) + sum(dot(bottom, j, nt) for j in tails2)
    ).reshape(4, 2, 4, 8, 128)

    cols = Reduce(
        exchange, x, z_lo, at_col, [xc], ([c_in1], [c_in2], [c_in3], [c_in4]), [wc]
    )
    rows = Reduce(
        exchange, y, z_hi, at_row, xr, (r_in1, r_in2, r_in3, r_in4), [w.at[core] for w in wr]
    )
    row_groups = range(len(ROW_GROUPS))

    def lanes(g):
        return slice(*ROW_GROUPS[g])

    cols.step1(0)

    across.wait_recv()
    j_pad[0:315, 0:630] = j_in[...]
    high, low = two_parts(spread_lanes(j_pad[...]))
    j_high[320:640, :] = high
    j_low[320:640, :] = low

    @pl.when(row != owner)
    def _():
        state_copies[0].wait_recv()

    rest = jnp.where(word_line < 6, states[...], 0.0)
    digits = []
    for _ in range(4):
        quotient = jnp.floor(rest * (1.0 / Q))
        remainder = rest - quotient * Q
        over, under = remainder >= Q, remainder < 0.0
        quotient = jnp.where(over, quotient + 1.0, jnp.where(under, quotient - 1.0, quotient))
        remainder = jnp.where(over, remainder - Q, jnp.where(under, remainder + Q, remainder))
        digits.append(remainder)
        rest = quotient
    digits = jnp.concatenate(digits + [rest], axis=0).astype(BF16)

    def digit_residue(shape, dim):
        at = iota(shape, dim)
        line = at % 8
        return jnp.where(line < 6, 5 * line + at // 8, -1)

    lane_b = iota((40, 640), 1)
    block_b = jnp.where(lane_b < 320, core, 1 - core)
    local_b = jnp.where(lane_b < 320, lane_b, lane_b - 320)
    spread_b = digit_residue((40, 640), 0) == block_b * 15 + residue_of(local_b)
    own_digits = jnp.where(core == 0, digits[:, 0:256].astype(F32), digits[:, 256:512].astype(F32))
    value_b = dot(own_digits.astype(BF16), as_bf16(spread_b), ((0,), (0,)))
    local = jnp.where(lane_r < 320, lane_r, lane_r - 320)
    hot_b = (value_b == (local - residue_of(local) * Q).astype(F32)) & (local < 315)
    hot_b = as_bf16(hot_b)
    for g in row_groups:
        at = lanes(g)
        sums = dot(hot_b, j_high[:, at]) + dot(hot_b, j_low[:, at])
        xr[g][...] = sums.reshape(4, 2, 4, 8, -1)
        rows.step1(g)

    lane_c = iota((1, 384), 1)
    spread_c = digit_residue((40, 384), 0) == core * 15 + residue_of(iota((40, 384), 1))
    value_c = dot(digits, as_bf16(spread_c), ((0,), (0,)))
    hot_c = (value_c == (lane_c - residue_of(lane_c) * Q).astype(F32)) & (lane_c < 315)
    oc32[...] = hot_c.astype(F32).reshape(64, 8, 384)
    line_c = iota((320, 1), 0)
    spread_t = digit_residue((320, 40), 1) == core * 15 + residue_of(iota((320, 40), 0))
    value_t = dot(as_bf16(spread_t), digits)
    hot_t = (value_t == (line_c - residue_of(line_c) * Q).astype(F32)) & (line_c < 315)
    hot_t = as_bf16(hot_t)
    oct[0] = hot_t[:, 0:256]
    oct[1] = hot_t[:, 256:512]

    cols.step2(0)
    for g in row_groups:
        rows.step2(g)
    cols.step3(0)
    for g in row_groups:
        rows.step3(g)
    for g in row_groups:
        rows.step4(g)
    cols.step4(0)

    def line_weights(first):
        lane = iota((8, 512), 1) - iota((8, 512), 0)
        found = [jnp.where(lane == first + 32 * h + 8 * i, w_ref[...], 0.0) for h, i in first_blocks]
        return jnp.sum(jnp.concatenate(found, axis=0), axis=1, keepdims=True)

    def residual(energy, hot, residue, weight):
        member = as_bf16(iota((128, energy.shape[1]), 0) == residue)
        powers = jnp.exp(energy)
        lines = energy.shape[0]
        parts = dot(jnp.concatenate(three_parts(powers), axis=0), member, nt)
        sums = parts[0:lines] + parts[lines : 2 * lines] + parts[2 * lines :]
        inverse = jnp.where(sums > 0.0, 1.0 / sums, 0.0)
        parts = dot(jnp.concatenate(three_parts(inverse), axis=0), member)
        inverse = parts[0:lines] + parts[lines : 2 * lines] + parts[2 * lines :]
        return weight * (powers * inverse - hot)

    column, second, valid = packed_column(lane_r)
    residue_c = jnp.where(valid, residue_of(column) + jnp.where(second, 32, 0), -1)
    first = x * 64
    first_blocks = cols.blocks()

    def column_lines(start):
        return jnp.concatenate([oc32[start // 8 + 4 * h + i] for h, i in cols.blocks()], axis=0)

    hot1, hot2 = column_lines(first), column_lines(first + 256)
    hot = jnp.concatenate(
        [hot1[:, 0:256], hot2[:, 0:256], hot1[:, 256:384] + pltpu.roll(hot2[:, 256:384], 64, 1)],
        axis=1,
    )
    fields_c = jnp.where(core == 0, states[6:7, :], states[7:8, :])
    f_main, f_tail = fields_c[:, 0:256], jnp.broadcast_to(fields_c[:, 256:384], (8, 128))
    f_tail = (f_tail + pltpu.roll(f_tail, 64, 1))[0:1]
    fields_c = jnp.concatenate([f_main, f_main, f_tail], axis=1)
    weight = jnp.where(second, line_weights(first + 256), line_weights(first))
    cols.gather1(0, residual(cols.result(0) + fields_c, hot, residue_c, weight))

    block = core * 32 + y * 8
    first_blocks = rows.blocks()
    weight = line_weights(core * 256 + y * 64)
    fields_r = spread_lanes(fpad[...])[0:1]
    for g in row_groups:
        low, high = ROW_GROUPS[g]
        at = lanes(g)
        hot = jnp.concatenate([or32[block + 4 * h + i, :, at] for h, i in rows.blocks()], axis=0)
        energy = rows.result(g) + fields_r[:, low:high]
        rows.gather1(g, residual(energy, hot, res_r[:, low:high], weight))
    cols.gather2(0)
    cols.gather3(0)
    for g in row_groups:
        rows.gather2(g)

    cols.gathered(0)
    whole = wc[...].reshape(256, 640)
    tail = whole[:, 512:640]
    tail_lane = iota((1, 128), 1)
    tail1 = jnp.where(tail_lane < 64, tail, 0.0)
    tail2 = pltpu.roll(jnp.where(tail_lane < 64, 0.0, tail), 64, 1)
    first_c = jnp.concatenate([whole[:, 0:256], tail1], axis=1)
    second_c = jnp.concatenate([whole[:, 256:512], tail2], axis=1)

    def products(n, lines):
        hot = or32[32 * n : 32 * n + 32].reshape(256, 640).astype(BF16)
        return sum(dot(piece, hot, ((0,), (0,))) for piece in two_parts(lines))

    acc[...] = products(0, first_c)
    last = {g: [] for g in row_groups}

    def forward(i, h, g):
        piece = wr[g].at[core, i, h]
        last[g].append(exchange(piece, piece, partner))

    for g in row_groups:
        rows.gather3(g)
        for h in range(2):
            forward(y, h, g)
            forward(order(y, h)[1], h, g)
    acc[...] += products(1, second_c)
    for g in row_groups:
        rows.gathered(g)
        for h in range(2):
            forward(order(y, h)[0], h, g)
            forward(far(y), h, g)

    for n, ref in enumerate((f_ref, fm_ref, fs_ref)):
        field_ref[n : n + 1, 0:630] = ref[...].reshape(1, 630)

    def row_products(which, g):
        lines = wr[g][which].reshape(256, -1)
        hot = oct[which]
        acc[0:320, lanes(g)] += sum(dot(hot, piece) for piece in two_parts(lines))
        return jnp.sum(lines, axis=0, keepdims=True)

    def finish(t):
        high = min(128 * t + 128, 630)
        tile = natural_tile(lambda i: acc[0:320, 128 * i : 128 * i + 128], t)
        g_ref[:, 128 * t : high] = tile[0:315, 0 : high - 128 * t]

    line_sums = [row_products(core, g) for g in row_groups]
    done = 0
    for g in row_groups:
        for copy in last[g]:
            copy.wait_recv()
        fg_ref[0:1, lanes(g)] = line_sums[g] + row_products(1 - core, g)
        ready = ROW_GROUPS[g][1] // 128
        for t in range(done, ready - (ready < 5)):
            finish(t)
        done = ready - 1

    def grad_tile(i):
        return fg_ref[:, 128 * i : 128 * i + 128]

    grad = jnp.concatenate([natural_tile(grad_tile, t) for t in range(5)], axis=1)
    field_ref[3:4, :] = grad[0:1]

    for load in loads[6:]:
        load.wait()
    for copy in copies[-SENDS:]:
        copy.wait_send()

    @pl.when(row == owner)
    def _():
        for copy in state_copies:
            copy.wait_send()


def adam_update(values, first_moment, second_moment, gradient):
    first_new = 0.9 * first_moment + 0.1 * gradient
    second_new = 0.999 * second_moment + 0.001 * gradient * gradient
    root = jnp.sqrt(second_new * (1.0 / (1.0 - 0.999**10)))
    change = first_new * (0.05 / (1.0 - 0.9**10)) / (root + 1e-08)
    return (values - change, first_new, second_new)


def on_device(
    alignment, seq_weight, couplings, pair_mean, pair_square, fields, field_mean, field_square
):
    vmem = pl.BlockSpec(memory_space=pltpu.VMEM)

    def by_group(*dims):
        return [pltpu.VMEM((*dims, high - low), F32) for low, high in ROW_GROUPS]

    sums, field_lines, held_mean, held_square = pl.pallas_call(
        kernel,
        out_shape=(
            jax.ShapeDtypeStruct(couplings.shape[::-1], F32),
            jax.ShapeDtypeStruct((4, 640), F32),
            *[jax.ShapeDtypeStruct(couplings.shape[::-1], F32)] * 2,
        ),
        in_specs=[pl.BlockSpec(memory_space=pltpu.HBM)] * 8,
        out_specs=(vmem,) * 4,
        scratch_shapes=[
            pltpu.VMEM((8, 512), F32),
            pltpu.VMEM((64, 8, 384), F32),
            pltpu.VMEM((64, 8, 640), F32),
            pltpu.VMEM((2, 320, 256), BF16),
            pltpu.VMEM((320, 640), F32),
            pltpu.VMEM((640, 640), BF16),
            pltpu.VMEM((640, 640), BF16),
            pltpu.VMEM(couplings.shape[::-1], F32),
        ]
        + [by_group(4, 2, 4, 8), pltpu.VMEM((4, 2, 4, 8, 640), F32)]
        + [by_group(2, 2, 4, 8), by_group(2, 4, 8), by_group(2, 2, 8), by_group(2, 2, 8)]
        + [
            pltpu.VMEM((2, 2, 4, 8, 640), F32),
            pltpu.VMEM((2, 4, 8, 640), F32),
            pltpu.VMEM((2, 2, 8, 640), F32),
            pltpu.VMEM((2, 2, 8, 640), F32),
            by_group(2, 4, 2, 4, 8),
            pltpu.VMEM((4, 2, 4, 8, 640), F32),
            pltpu.VMEM((384, 640), F32),
            pltpu.VMEM((8, 640), F32),
            pltpu.VMEM((8, 640), F32),
            pltpu.VMEM(alignment.shape[::-1], jnp.int32),
            pltpu.VMEM((1, 512), F32),
            pltpu.VMEM(couplings.shape[::-1], F32),
            *[pltpu.VMEM(fields.shape, F32)] * 3,
            pltpu.SemaphoreType.DMA((8,)),
            pltpu.SemaphoreType.DMA((16,)),
            pltpu.SemaphoreType.DMA((SENDS,)),
            pltpu.SemaphoreType.DMA((20 + 26 * len(ROW_GROUPS),)),
        ],
        compiler_params=pltpu.CompilerParams(collective_id=0, has_side_effects=True, vmem_limit_bytes=VMEM_LIMIT),
    )(*(
        pltpu.with_memory_space_constraint(x, pltpu.HBM)
        for x in (
            alignment.T, seq_weight.reshape(1, -1), couplings.T,
            fields, field_mean, field_square, pair_mean.T, pair_square.T,
        )
    ))
    pair_mean, pair_square = held_mean.T, held_square.T
    sums = sums.T
    row_residues = alignment.shape[1]
    column_residues = couplings.shape[1] // Q
    row_ids = (
        lax.axis_index("row") * row_residues
        + lax.broadcasted_iota(jnp.int32, (couplings.shape[0], 1), 0) // Q
    )
    column_ids = (
        lax.axis_index("col") * column_residues
        + lax.broadcasted_iota(jnp.int32, (1, couplings.shape[1]), 1) // Q
    )
    pair_grad = jnp.where(row_ids != column_ids, sums, 0.0) + 0.2 * (L - 1) * couplings
    new_pairs, new_pair_mean, new_pair_square = adam_update(
        couplings, pair_mean, pair_square, pair_grad
    )
    new_fields, new_field_mean, new_field_square = adam_update(
        *(field_lines[n, : fields.shape[0]] for n in range(4))
    )
    return (new_pairs, new_pair_mean, new_pair_square, new_fields, new_field_mean, new_field_square)


def solution(mesh):
    block = P("row", "col")
    in_specs = (P(None, "row"), P(), block, block, block, P("row"), P("row"), P("row"))
    out_specs = (block, block, block, P("row"), P("row"), P("row"))
    return jax.shard_map(
        on_device, mesh=mesh, in_specs=in_specs, out_specs=out_specs, check_vma=False
    )
```
